256 devices in a mesh: replica: 4 (over z_lo), shard: 64 (over y, z_hi, x, core).
Axes of the slice: x: 4, y: 4, z: 8 (z_hi: 2, z_lo: 4; z = z_hi * 4 + z_lo), core: 2. Of those that a mesh axis runs over, the one named last changes fastest.
Arguments:
- activations: bfloat16 [32768, 512], P(('replica', 'shard')), may hold values from -6 to 6
- cotangents: bfloat16 [32768, 8192], P(('replica', 'shard')), may hold values from -0.005859375 to 0.005859375
- statistics: float32 [2, 8192, 512], P(None, 'shard'), may hold values from -8 to 32, as said below
- roots: bfloat16 [2, 8192, 512], P(None, 'shard'), may hold values from -0.25 to 0.25
- ages: int32 [32], replicated, may hold values from 1 to 16
- refresh: int32 [32], replicated, may hold values 0 or 1
Outputs:
- update: bfloat16 [8192, 512], P('shard')
- new_statistics: float32 [2, 8192, 512], P(None, 'shard')
- new_roots: bfloat16 [2, 8192, 512], P(None, 'shard')
The draws below stay inside these ranges and needn't reach their ends.
Inputs may be any that keep to these rules, and one draw needn't show every extreme that they name: `statistics`: for each block k, rows k * 512 to (k + 1) * 512 - 1 of either layer hold a symmetric positive definite 512 x 512 matrix.
All inputs are finite; a program needn't handle non-finite values.
Results may differ from the reference program's by a relative error of at most 0.0064.
Values may be sent and summed in bfloat16 or wider, within the bound.
No kernel may reach another device: no remote copies, remote signals or barrier semaphores. Data moves between devices by JAX's collectives and lax.ppermute only.
A program may use at most 128 MiB of HBM per device.

```python
import math
import jax
import jax.numpy as jnp
from jax import lax

D = 8192
B = 512
ITERS = 3
TOKENS = 32768
FACTORS = 32


def draw_statistics(key, part):
    base_key = jax.random.fold_in(key, 11)
    scale_key = jax.random.fold_in(key, 12)
    entries = jax.random.normal(base_key, (2, D // B, B, B), jnp.float32)
    spread = jnp.exp(jax.random.uniform(scale_key, (2, D // B, B), jnp.float32, 0.0, math.log(3.0)))
    inner_form = jnp.einsum('kbij,kblj->kbil', entries, entries, precision=lax.Precision.HIGHEST) / B
    inner_form = inner_form + 0.5 * jnp.eye(B, dtype=jnp.float32)
    blocks_full = spread[..., :, None] * inner_form * spread[..., None, :]
    return blocks_full.reshape(2, D, B)


def with_ends(result, stream_key, least, high):
    extent = result.shape
    place = [jax.random.randint(jax.random.fold_in(stream_key, axis), (), 0, extent[axis]) for axis in range(len(extent))]
    result = result.at[tuple(place)].set(least)
    longest = extent.index(max(extent))
    place[longest] = (place[longest] + 1) % extent[longest]
    return result.at[tuple(place)].set(high)


def with_spikes(drawn, stream_key, source, target, shards_of, factor):
    def block_of(position):
        return (jnp.arange(drawn.shape[position]) // (drawn.shape[position] // shards_of)).reshape((-1,) + (1,) * (drawn.ndim - 1 - position))

    one_side = jax.random.permutation(stream_key, shards_of)[block_of(target)]
    other_side = (block_of(target) + shards_of // 2) % shards_of
    return jnp.where((block_of(source) == one_side) | (block_of(source) == other_side), factor * drawn, drawn)


def block_levels(own_key, shape, split, least, high):
    level = 1.0
    for dim, blocks in split:
        draws = jax.random.uniform(jax.random.fold_in(jax.random.fold_in(own_key, 6), dim), (blocks,), jnp.float32, least / len(split), high / len(split))
        level = level * jnp.repeat(jnp.exp(draws), shape[dim] // blocks).reshape((-1,) + (1,) * (len(shape) - 1 - dim))
    return level


def scatter_about(rng, extent, scale, bound, pieces=(), kind=jnp.bfloat16):
    gain = block_levels(rng, extent, pieces, -0.22, 0.18) if pieces else 1.0
    array = jax.random.normal(rng, extent, jnp.float32) * scale * gain
    return jnp.minimum(jnp.maximum(array, -bound), bound).astype(kind)


def noise_with(rng, shape, scale, reach, pieces, heavy, kind=jnp.bfloat16):
    drawn = scale * jax.random.normal(rng, shape, jnp.float32)
    if pieces:
        drawn = drawn * block_levels(rng, shape, pieces, -0.22, 0.18)
    return jnp.clip(with_spikes(drawn, jax.random.fold_in(rng, 3), *heavy), -reach, reach).astype(kind)


def setup_inputs(seed: int = 0) -> dict:
    splits = jax.random.split(jax.random.key(seed), 7)
    activations = scatter_about(splits[0], (TOKENS, B), 1.0, 6.0, ((0, 256),))
    cotangents = noise_with(splits[1], (TOKENS, D), (TOKENS * B) ** -0.5, 0.005859375, ((0, 256),), (0, 1, 256, 6.0))
    statistics = draw_statistics(jax.random.fold_in(splits[6], 71), 0)
    roots = scatter_about(splits[3], (2, D, B), B ** -0.5, 0.25, ((1, 64),))
    ages = with_ends(jax.random.randint(splits[4], (FACTORS,), 1, 17), jax.random.fold_in(splits[4], 1), 1, 16).astype(jnp.int32)
    refresh = with_ends((jax.random.randint(splits[5], (FACTORS,), 0, 2) < 1).astype(jnp.int32), jax.random.fold_in(splits[5], 1), 0, 1)
    return {"activations": activations, "cotangents": cotangents, "statistics": statistics, "roots": roots, "ages": ages, "refresh": refresh}


decay_base = 0.9
tiny_term = 1e-06

def newton(matrix):
    identity = jnp.eye(matrix.shape[-1], dtype=jnp.float32)
    frobenius = jnp.sqrt(jnp.sum(matrix * matrix) + tiny_term)
    scaling = 2.5 / frobenius
    iterate = scaling ** 0.25 * identity
    residual_map = scaling * matrix
    for sweep_index in range(ITERS):
        factor = (5.0 * identity - residual_map) * 0.25
        iterate = jnp.matmul(iterate, factor, precision=lax.Precision.HIGHEST)
        square = jnp.matmul(factor, factor, precision=lax.Precision.HIGHEST)
        fourth = jnp.matmul(square, square, precision=lax.Precision.HIGHEST)
        residual_map = jnp.matmul(fourth, residual_map, precision=lax.Precision.HIGHEST)
    return iterate

def reference(activations, cotangents, statistics, roots, ages, refresh):
    block_count = D // B
    gradient = lax.dot_general(cotangents, activations, (((0,), (0,)), ((), ())), preferred_element_type=jnp.float32)
    grad_blocks = gradient.astype(jnp.bfloat16).reshape(block_count, B, B)
    wide_blocks = grad_blocks.astype(jnp.float32)
    left_gram = jnp.einsum('nij,nkj->nik', wide_blocks, wide_blocks, precision=lax.Precision.HIGHEST)
    right_gram = jnp.einsum('nji,njk->nik', wide_blocks, wide_blocks, precision=lax.Precision.HIGHEST)
    gram_pairs = jnp.stack([left_gram, right_gram], axis=1).reshape(2 * block_count, B, B)
    previous = statistics.reshape(2, block_count, B, B).transpose(1, 0, 2, 3).reshape(2 * block_count, B, B)
    decay_factor = (decay_base ** ages.astype(jnp.float32))[:, None, None]
    fresh_mask = (refresh == 1)[:, None, None]
    updated = jnp.where(fresh_mask, decay_factor * previous + (1.0 - decay_factor) * gram_pairs, previous)
    fresh_roots = lax.map(newton, updated).astype(jnp.bfloat16)
    old_roots = roots.reshape(2, block_count, B, B).transpose(1, 0, 2, 3).reshape(2 * block_count, B, B)
    root_all = jnp.where(fresh_mask, fresh_roots, old_roots).reshape(block_count, 2, B, B)
    left_roots = root_all[:, 0].astype(jnp.float32)
    right_roots = root_all[:, 1].astype(jnp.float32)
    mixed_blocks = jnp.einsum('nij,njk->nik', wide_blocks, right_roots, precision=lax.Precision.HIGHEST).astype(jnp.bfloat16)
    product = jnp.einsum('nij,njk->nik', left_roots, mixed_blocks.astype(jnp.float32), precision=lax.Precision.HIGHEST)
    update = (product * math.sqrt(B)).reshape(D, B).astype(jnp.bfloat16)
    new_statistics = updated.reshape(block_count, 2, B, B).transpose(1, 0, 2, 3).reshape(2, D, B)
    new_roots = root_all.transpose(1, 0, 2, 3).reshape(2, D, B)
    return (update, new_statistics, new_roots)
```

```python
import math

import jax
import jax.numpy as jnp
from jax import lax
from jax.experimental import pallas as pl
from jax.experimental.pallas import tpu as pltpu
from jax.sharding import Mesh
from jax.sharding import PartitionSpec as P

X = ("x_hi", "x_lo")
Z = ("z_lo", "z_hi")
SHARD = ("y", "z_hi", "x_hi", "x_lo", "core")
EVERY = ("z_lo",) + SHARD

B = 512
ROWS = 128
PART = 32
SEND = jnp.bfloat16

decay_base = 0.9
tiny_term = 1e-06


def shift(x, axis, by):
    n = lax.axis_size(axis)
    return lax.ppermute(x, axis, [(i, (i + by) % n) for i in range(n)])


def shift_z(x, by):
    spot = [(i % 4) * 2 + i // 4 for i in range(8)]
    return lax.ppermute(x, Z, [(spot[i], spot[(i + by) % 8]) for i in range(8)])


def partner(x, axis, bits=1):
    n = lax.axis_size(axis)
    return lax.ppermute(x, axis, [(i, i ^ bits) for i in range(n)])


def pick(x, index):
    return lax.dynamic_index_in_dim(x, index, 0, keepdims=False)


def dot(a, b, contract=(1, 0)):
    dims = (((contract[0],), (contract[1],)), ((), ()))
    return lax.dot_general(a, b, dims, preferred_element_type=jnp.float32)


def narrow(x):
    return x.astype(jnp.bfloat16)


def finish_kernel(place, fresh, decay, pieces, stats, right_old, left_old,
                  update, new_stats, new_roots, grad, full, right, work):
    x_lo, core, z_lo = place[0], place[1], place[2]
    quarter = x_lo * 2 + core
    own = pl.ds(pl.multiple_of(quarter * ROWS, ROWS), ROWS)
    for a in range(2):
        for b in range(2):
            top = ((x_lo ^ a) * 2 + (core ^ b)) * ROWS
            here = pl.ds(pl.multiple_of(top, ROWS), ROWS)
            right[here, :] = right_old[b, a]
            for layer in range(2):
                full[layer, here, :] = stats[b, a, layer]
            for k in range(4):
                rows = pl.multiple_of(top + (z_lo ^ k) * PART, PART)
                grad[pl.ds(rows, PART), :] = pieces[b, a, k]
    g = grad[...]

    def refresh_stats(layer, gram):
        old = full[layer]
        d = decay[layer]
        a = jnp.where(fresh[layer] == 1, d * old + (1.0 - d) * gram, old)
        full[layer] = a
        new_stats[layer] = full[layer, own, :]
        total = jnp.sum(jnp.sum(a * a, axis=0, keepdims=True), axis=1, keepdims=True)
        scaling = 2.5 / jnp.sqrt(total + tiny_term)
        return scaling * a, jnp.sqrt(jnp.sqrt(scaling))

    def advance(m):
        mb = narrow(m)
        u = narrow(dot(mb, mb) * 0.0625 - 0.625 * m)
        w = dot(u, mb)
        return 2.44140625 * m + 3.125 * w + dot(u, narrow(w))

    def root_of(m, m_rows, m2, m2_rows, m3, m3_rows, row0, scale):
        y = dot(narrow(m_rows), narrow(m2)) * 0.0625 - 0.3125 * (m_rows + m2_rows)
        r = lax.broadcasted_iota(jnp.int32, m_rows.shape, 0) + row0
        c = lax.broadcasted_iota(jnp.int32, m_rows.shape, 1)
        out = jnp.where(r == c, 1.953125, 0.0) + 1.25 * y - 0.390625 * m3_rows
        out = out - 0.25 * dot(narrow(y), narrow(m3))
        return narrow(scale * out)

    m, scale = refresh_stats(1, dot(g, g, (0, 0)))
    m2 = advance(m)
    m3 = advance(m2)
    root = root_of(m, m, m2, m2, m3, m3, 0, scale)
    root = jnp.where(fresh[1] == 1, root, right[...])
    right[...] = root
    new_roots[1] = right[own, :]
    mixed = narrow(dot(g, root))

    m, scale = refresh_stats(0, dot(g, g, (1, 1)))
    work[0] = m
    m2 = advance(m)
    work[1] = m2
    m3 = advance(m2)
    work[2] = m3
    rows = root_of(m, work[0, own, :], m2, work[1, own, :], m3, work[2, own, :], quarter * ROWS, scale)
    rows = jnp.where(fresh[0] == 1, rows, left_old[...])
    new_roots[0] = rows
    update[...] = narrow(dot(rows, mixed) * math.sqrt(B))


def finish(place, fresh, decay, pieces, stats, right_old, left_old):
    smem = pl.BlockSpec(memory_space=pltpu.SMEM)
    vmem = pl.BlockSpec(memory_space=pltpu.VMEM)
    return pl.pallas_call(
        finish_kernel,
        name="finish",
        out_shape=(
            jax.ShapeDtypeStruct((ROWS, B), jnp.bfloat16),
            jax.ShapeDtypeStruct((2, ROWS, B), jnp.float32),
            jax.ShapeDtypeStruct((2, ROWS, B), jnp.bfloat16),
        ),
        in_specs=[smem] * 3 + [vmem] * 4,
        out_specs=(vmem,) * 3,
        scratch_shapes=[
            pltpu.VMEM((B, B), jnp.bfloat16),
            pltpu.VMEM((2, B, B), jnp.float32),
            pltpu.VMEM((B, B), jnp.bfloat16),
            pltpu.VMEM((3, B, B), jnp.float32),
        ],
        compiler_params=pltpu.CompilerParams(vmem_limit_bytes=40 << 20),
        cost_estimate=pl.CostEstimate(flops=18 * 2 * B**3, bytes_accessed=6 << 20, transcendentals=0),
    )(place, fresh, decay, pieces, stats, right_old, left_old)


def per_device(activations, cotangents, statistics, roots, ages, refresh):
    x, y = lax.axis_index(X), lax.axis_index("y")
    x_hi, x_lo, z_hi, z_lo = (lax.axis_index(a) for a in ("x_hi", "x_lo", "z_hi", "z_lo"))
    core = lax.axis_index("core")
    z = z_hi * 4 + z_lo

    def y_piece(t):
        columns = lax.dynamic_slice_in_dim(cotangents, t * 4 * B, 2 * B, 1)
        return jnp.concatenate([columns, activations], axis=1)

    def x_piece(t):
        columns = [
            lax.dynamic_slice_in_dim(cotangents, (4 * j + 2) * B + t * B // 2, B // 2, 1)
            for j in range(4)
        ]
        return jnp.concatenate(columns + [activations], axis=1)

    def product(pieces):
        both = jnp.concatenate(pieces, axis=0)
        return dot(both[:, : 2 * B], both[:, 2 * B :], (0, 0))

    y_parts, x_parts = [y_piece(y)], [x_piece(x)]
    for k in (2, 1, 3):
        y_parts.append(shift(y_piece((y + k) % 4), "y", k))
        x_parts.append(shift(x_piece((x + k) % 4), X, k))

    def core_sum(total):
        halves = total.reshape(4, 2, ROWS, B).swapaxes(0, 1)
        return pick(halves, core) + partner(pick(halves, 1 - core), "core")

    y_sum = core_sum(product(y_parts))
    x_sum = core_sum(product(x_parts))
    y_total, x_total = pick(y_sum, x), pick(x_sum, y)
    for k in (2, 1, 3):
        y_total += shift(pick(y_sum, (x + k) % 4).astype(SEND), X, k).astype(jnp.float32)
        x_total += shift(pick(x_sum, (y + k) % 4).astype(SEND), "y", k).astype(jnp.float32)

    plane = jnp.stack([y_total, x_total]).reshape(8, PART, B)
    plane, statistics, roots = lax.optimization_barrier((plane, statistics, roots))
    part = pick(plane, z)
    for k in (4, 3, 5, 2, 6, 1, 7):
        part += shift_z(pick(plane, (z + k) % 8).astype(SEND), k).astype(jnp.float32)
    part = narrow(part)
    pieces = jnp.stack([part] + [partner(part, "z_lo", k) for k in (1, 2, 3)])
    pieces = jnp.stack([pieces, partner(pieces, "x_lo")])
    pieces = jnp.stack([pieces, partner(pieces, "core")])

    stats = jnp.stack([statistics, partner(statistics, "x_lo")])
    stats = jnp.stack([stats, partner(stats, "core")])
    right_old = jnp.stack([roots[1], partner(roots[1], "x_lo")])
    right_old = jnp.stack([right_old, partner(right_old, "core")])

    block = y * 4 + z_hi * 2 + x_hi
    ages_here = lax.dynamic_slice_in_dim(ages, 2 * block, 2, 0)
    fresh = lax.dynamic_slice_in_dim(refresh, 2 * block, 2, 0)
    decay = decay_base ** ages_here.astype(jnp.float32)
    place = jnp.stack([x_lo, core, z_lo]).astype(jnp.int32)
    return finish(place, fresh, decay, pieces, stats, right_old, roots[0])


def solution(mesh):
    split = Mesh(mesh.devices.reshape(4, 4, 2, 2, 2, 2), EVERY)
    placed = (P(EVERY, None), P(EVERY, None), P(None, SHARD, None), P(None, SHARD, None), P(), P())
    return jax.shard_map(
        per_device,
        mesh=split,
        in_specs=placed,
        out_specs=(P(SHARD, None), P(None, SHARD, None), P(None, SHARD, None)),
        check_vma=False,
    )
```

```python
import math

import jax
import jax.numpy as jnp
from jax import lax
from jax.experimental import pallas as pl
from jax.experimental.pallas import tpu as pltpu
from jax.sharding import Mesh
from jax.sharding import PartitionSpec as P

X = ("x_hi", "x_lo")
Z = ("z_lo", "z_hi")
SHARD = ("y", "z_hi", "x_hi", "x_lo", "core")
EVERY = ("z_lo",) + SHARD

B = 512
ROWS = 128
TOKENS = 128
WIDE = 3 * B
SEND = jnp.bfloat16

decay_base = 0.9
tiny_term = 1e-06


def shift(x, axis, by):
    n = lax.axis_size(axis)
    return lax.ppermute(x, axis, [(i, (i + by) % n) for i in range(n)])


def swap_z(x, bits):
    spot = [(i % 4) * 2 + i // 4 for i in range(8)]
    return lax.ppermute(x, Z, [(spot[i], spot[i ^ bits]) for i in range(8)])


def partner(x, axis, bits=1):
    n = lax.axis_size(axis)
    return lax.ppermute(x, axis, [(i, i ^ bits) for i in range(n)])


def dot(a, b, contract=(1, 0)):
    dims = (((contract[0],), (contract[1],)), ((), ()))
    return lax.dot_general(a, b, dims, preferred_element_type=jnp.float32)


def narrow(x):
    return x.astype(jnp.bfloat16)


def rounded(x):
    return lax.optimization_barrier(narrow(x))


def finish_kernel(place, fresh, decay, g0, g1, g2, g3, s0, s1, s2, s3, r0, r1, r2, r3, left_old,
                  update, new_stats, new_roots, grad, full, right, work):
    x_lo, core = place[0], place[1]
    pieces, stats, right_old = (g0, g1, g2, g3), (s0, s1, s2, s3), (r0, r1, r2, r3)
    quarter = x_lo * 2 + core
    own = pl.ds(pl.multiple_of(quarter * ROWS, ROWS), ROWS)
    for a in range(2):
        for b in range(2):
            top = ((x_lo ^ a) * 2 + (core ^ b)) * ROWS
            here = pl.ds(pl.multiple_of(top, ROWS), ROWS)
            right[here, :] = right_old[2 * b + a][...]
            grad[here, :] = pieces[2 * b + a][...]
            for layer in range(2):
                full[layer, here, :] = stats[2 * b + a][layer]
    g = grad[...]

    def refresh_stats(layer, gram):
        old = full[layer]
        d = decay[layer]
        a = jnp.where(fresh[layer] == 1, d * old + (1.0 - d) * gram, old)
        full[layer] = a
        new_stats[layer] = full[layer, own, :]
        total = jnp.sum(jnp.sum(a * a, axis=0, keepdims=True), axis=1, keepdims=True)
        scaling = 2.5 / jnp.sqrt(total + tiny_term)
        return scaling * a, jnp.sqrt(jnp.sqrt(scaling))

    def advance(m):
        mb = narrow(m)
        u = narrow(dot(mb, mb) * 0.0625 - 0.625 * m)
        w = dot(u, mb)
        return 2.44140625 * m + 3.125 * w + dot(u, narrow(w))

    def root_of(m, m_rows, m2, m2_rows, m3, m3_rows, row0, scale):
        y = dot(narrow(m_rows), narrow(m2)) * 0.0625 - 0.3125 * (m_rows + m2_rows)
        r = lax.broadcasted_iota(jnp.int32, m_rows.shape, 0) + row0
        c = lax.broadcasted_iota(jnp.int32, m_rows.shape, 1)
        out = jnp.where(r == c, 1.953125, 0.0) + 1.25 * y - 0.390625 * m3_rows
        out = out - 0.25 * dot(narrow(y), narrow(m3))
        return narrow(scale * out)

    m, scale = refresh_stats(1, dot(g, g, (0, 0)))
    m2 = advance(m)
    m3 = advance(m2)
    root = root_of(m, m, m2, m2, m3, m3, 0, scale)
    root = jnp.where(fresh[1] == 1, root, right[...])
    right[...] = root
    new_roots[1] = right[own, :]
    mixed = narrow(dot(g, root))

    m, scale = refresh_stats(0, dot(g, g, (1, 1)))
    work[0] = m
    m2 = advance(m)
    work[1] = m2
    m3 = advance(m2)
    work[2] = m3
    rows = root_of(m, work[0, own, :], m2, work[1, own, :], m3, work[2, own, :], quarter * ROWS, scale)
    rows = jnp.where(fresh[0] == 1, rows, left_old[...])
    new_roots[0] = rows
    update[...] = narrow(dot(rows, mixed) * math.sqrt(B))


def finish(place, fresh, decay, *arrays):
    smem = pl.BlockSpec(memory_space=pltpu.SMEM)
    vmem = pl.BlockSpec(memory_space=pltpu.VMEM)
    return pl.pallas_call(
        finish_kernel,
        name="finish",
        out_shape=(
            jax.ShapeDtypeStruct((ROWS, B), jnp.bfloat16),
            jax.ShapeDtypeStruct((2, ROWS, B), jnp.float32),
            jax.ShapeDtypeStruct((2, ROWS, B), jnp.bfloat16),
        ),
        in_specs=[smem] * 3 + [vmem] * 13,
        out_specs=(vmem,) * 3,
        scratch_shapes=[
            pltpu.VMEM((B, B), jnp.bfloat16),
            pltpu.VMEM((2, B, B), jnp.float32),
            pltpu.VMEM((B, B), jnp.bfloat16),
            pltpu.VMEM((3, B, B), jnp.float32),
        ],
        compiler_params=pltpu.CompilerParams(vmem_limit_bytes=40 << 20),
        cost_estimate=pl.CostEstimate(flops=18 * 2 * B**3, bytes_accessed=6 << 20, transcendentals=0),
    )(place, fresh, decay, *arrays)


def cut_kernel(place, cotangents, activations, *rest):
    outs, sem = rest[:-1], rest[-1]
    copies = []

    def copy(src, dst):
        copies.append(pltpu.make_async_copy(src, dst, sem.at[len(copies)]))
        copies[-1].start()

    for k, out in zip((2, 1, 3, 0), outs[0::2]):
        t = lax.rem(place[0] + k, 4)
        copy(cotangents.at[:, pl.ds(pl.multiple_of(t * 4 * B, 4 * B), 2 * B)], out.at[:, : 2 * B])
        copy(activations, out.at[:, 2 * B :])
    for k, out in zip((2, 1, 3, 0), outs[1::2]):
        t = lax.rem(place[1] + k, 4)
        for j in range(4):
            start = pl.multiple_of(t * (B // 2) + (4 * j + 2) * B, B // 2)
            copy(cotangents.at[:, pl.ds(start, B // 2)], out.at[:, j * (B // 2) : (j + 1) * (B // 2)])
        copy(activations, out.at[:, 2 * B :])
    for c in copies:
        c.wait()


def cut(place, cotangents, activations):
    free = pl.BlockSpec(memory_space=pl.ANY)
    return pl.pallas_call(
        cut_kernel,
        name="cut",
        out_shape=(jax.ShapeDtypeStruct((TOKENS, WIDE), jnp.bfloat16),) * 8,
        in_specs=[pl.BlockSpec(memory_space=pltpu.SMEM), free, free],
        out_specs=(free,) * 8,
        scratch_shapes=[pltpu.SemaphoreType.DMA((28,))],
        cost_estimate=pl.CostEstimate(flops=0, bytes_accessed=6 << 20, transcendentals=0),
    )(place, cotangents, activations)


def product_kernel(core, p0, p1, p2, p3, keep, send):
    parts = (p0, p1, p2, p3)
    right = jnp.concatenate([p[:, 2 * B :] for p in parts], axis=0)
    for out, side in ((send, 1 - core[0]), (keep, core[0])):
        left = jnp.concatenate(
            [
                jnp.concatenate(
                    [p[:, pl.ds(pl.multiple_of((2 * g + side) * ROWS, ROWS), ROWS)] for g in range(4)], axis=1
                )
                for p in parts
            ],
            axis=0,
        )
        out[...] = dot(left, right, (0, 0)).reshape(4, ROWS, B).astype(out.dtype)


def product(core, parts):
    vmem = pl.BlockSpec(memory_space=pltpu.VMEM)
    return pl.pallas_call(
        product_kernel,
        name="product",
        out_shape=(
            jax.ShapeDtypeStruct((4, ROWS, B), jnp.float32),
            jax.ShapeDtypeStruct((4, ROWS, B), SEND),
        ),
        in_specs=[pl.BlockSpec(memory_space=pltpu.SMEM)] + [vmem] * 4,
        out_specs=(vmem,) * 2,
        compiler_params=pltpu.CompilerParams(vmem_limit_bytes=24 << 20),
        cost_estimate=pl.CostEstimate(flops=4 * B**3, bytes_accessed=3 << 20, transcendentals=0),
    )(core, *parts)


def core_sum_kernel(place, keep, came, own, *sends):
    for k, out in zip((0, 2, 1, 3), (own,) + sends):
        t = lax.rem(place[0] + k, 4)
        out[...] = (keep[t] + came[t].astype(jnp.float32)).astype(out.dtype)


def core_sum(place, keep, came):
    vmem = pl.BlockSpec(memory_space=pltpu.VMEM)
    return pl.pallas_call(
        core_sum_kernel,
        name="core_sum",
        out_shape=(jax.ShapeDtypeStruct((ROWS, B), jnp.float32),) + (jax.ShapeDtypeStruct((ROWS, B), SEND),) * 3,
        in_specs=[pl.BlockSpec(memory_space=pltpu.SMEM)] + [vmem] * 2,
        out_specs=(vmem,) * 4,
        cost_estimate=pl.CostEstimate(flops=4 * ROWS * B, bytes_accessed=2 << 20, transcendentals=0),
    )(place, keep, came)


def per_device(activations, cotangents, statistics, roots, ages, refresh):
    x, y = lax.axis_index(X), lax.axis_index("y")
    x_hi, x_lo, z_hi, z_lo = (lax.axis_index(a) for a in ("x_hi", "x_lo", "z_hi", "z_lo"))
    core = lax.axis_index("core")

    def scalars(*values):
        return jnp.stack(values).astype(jnp.int32)

    pieces = cut(scalars(y, x), cotangents, activations)
    y_parts, x_parts = [pieces[6]], [pieces[7]]
    for i, k in enumerate((2, 1, 3)):
        y_parts.append(shift(pieces[2 * i], "y", k))
        x_parts.append(shift(pieces[2 * i + 1], X, k))
    stats_core, right_core = partner(statistics, "core"), partner(roots[1], "core")

    y_keep, y_send = product(scalars(core), y_parts)
    y_came = partner(y_send, "core")
    x_keep, x_send = product(scalars(core), x_parts)
    x_came = partner(x_send, "core")
    y_total, *y_sends = core_sum(scalars(x), y_keep, y_came)
    x_total, *x_sends = core_sum(scalars(y), x_keep, x_came)
    for i, k in enumerate((2, 1, 3)):
        y_total += shift(y_sends[i], X, k).astype(jnp.float32)
        x_total += shift(x_sends[i], "y", k).astype(jnp.float32)

    keep = jnp.where(z_hi == 0, y_total, x_total)
    send = jnp.where(z_hi == 0, x_total, y_total).astype(SEND)
    keep, send, statistics, right = lax.optimization_barrier((keep, send, statistics, roots[1]))
    part = rounded(keep + swap_z(send, 7).astype(jnp.float32))
    stats_x, right_x = partner(statistics, "x_lo"), partner(right, "x_lo")
    part = rounded(part.astype(jnp.float32) + swap_z(part, 1).astype(jnp.float32))
    part = rounded(part.astype(jnp.float32) + swap_z(part, 2).astype(jnp.float32))
    part_x, part_core = partner(part, "x_lo"), partner(part, "core")
    grads = (part, part_x, part_core, partner(part_x, "core"))
    stats = (statistics, stats_x, stats_core, partner(stats_x, "core"))
    rights = (right, right_x, right_core, partner(right_x, "core"))

    block = y * 4 + z_hi * 2 + x_hi
    ages_here = lax.dynamic_slice_in_dim(ages, 2 * block, 2, 0)
    fresh = lax.dynamic_slice_in_dim(refresh, 2 * block, 2, 0)
    decay = decay_base ** ages_here.astype(jnp.float32)
    return finish(scalars(x_lo, core), fresh, decay, *grads, *stats, *rights, roots[0])


def solution(mesh):
    split = Mesh(mesh.devices.reshape(4, 4, 2, 2, 2, 2), EVERY)
    placed = (P(EVERY, None), P(EVERY, None), P(None, SHARD, None), P(None, SHARD, None), P(), P())
    return jax.shard_map(
        per_device,
        mesh=split,
        in_specs=placed,
        out_specs=(P(SHARD, None), P(None, SHARD, None), P(None, SHARD, None)),
        check_vma=False,
    )
```

```python
import math

import jax
import jax.numpy as jnp
from jax import lax
from jax.experimental import pallas as pl
from jax.experimental.pallas import tpu as pltpu
from jax.sharding import Mesh
from jax.sharding import PartitionSpec as P

X = ("x_hi", "x_lo")
Z = ("z_lo", "z_hi")
SHARD = ("y", "z_hi", "x_hi", "x_lo", "core")
EVERY = ("z_lo",) + SHARD

B = 512
ROWS = 128
TOKENS = 128
WIDE = 3 * B
SEND = jnp.bfloat16

decay_base = 0.9
tiny_term = 1e-06


def shift(x, axis, by):
    n = lax.axis_size(axis)
    return lax.ppermute(x, axis, [(i, (i + by) % n) for i in range(n)])


def swap_z(x, bits):
    spot = [(i % 4) * 2 + i // 4 for i in range(8)]
    return lax.ppermute(x, Z, [(spot[i], spot[i ^ bits]) for i in range(8)])


def partner(x, axis, bits=1):
    n = lax.axis_size(axis)
    return lax.ppermute(x, axis, [(i, i ^ bits) for i in range(n)])


def dot(a, b, contract=(1, 0)):
    dims = (((contract[0],), (contract[1],)), ((), ()))
    return lax.dot_general(a, b, dims, preferred_element_type=jnp.float32)


def narrow(x):
    return x.astype(jnp.bfloat16)


def rounded(x):
    return lax.optimization_barrier(narrow(x))


def finish_kernel(place, fresh, decay, g0, g1, g2, g3, s0, s1, s2, s3, r0, r1, r2, r3, left_old,
                  update, new_stats, new_roots, grad, full, right, work):
    x_lo, core = place[0], place[1]
    pieces, stats, right_old = (g0, g1, g2, g3), (s0, s1, s2, s3), (r0, r1, r2, r3)
    quarter = x_lo * 2 + core
    own = pl.ds(pl.multiple_of(quarter * ROWS, ROWS), ROWS)
    for a in range(2):
        for b in range(2):
            top = ((x_lo ^ a) * 2 + (core ^ b)) * ROWS
            here = pl.ds(pl.multiple_of(top, ROWS), ROWS)
            right[here, :] = right_old[2 * b + a][...]
            grad[here, :] = pieces[2 * b + a][...]
            for layer in range(2):
                full[layer, here, :] = stats[2 * b + a][layer]
    g = grad[...]

    def refresh_stats(layer, gram):
        old = full[layer]
        d = decay[layer]
        a = jnp.where(fresh[layer] == 1, d * old + (1.0 - d) * gram, old)
        full[layer] = a
        new_stats[layer] = full[layer, own, :]
        total = jnp.sum(jnp.sum(a * a, axis=0, keepdims=True), axis=1, keepdims=True)
        scaling = 2.5 / jnp.sqrt(total + tiny_term)
        return scaling * a, jnp.sqrt(jnp.sqrt(scaling))

    def advance(m):
        mb = narrow(m)
        u = narrow(dot(mb, mb) * 0.0625 - 0.625 * m)
        w = dot(u, mb)
        return 2.44140625 * m + 3.125 * w + dot(u, narrow(w))

    def root_of(m, m_rows, m2, m2_rows, m3, m3_rows, row0, scale):
        y = dot(narrow(m_rows), narrow(m2)) * 0.0625 - 0.3125 * (m_rows + m2_rows)
        r = lax.broadcasted_iota(jnp.int32, m_rows.shape, 0) + row0
        c = lax.broadcasted_iota(jnp.int32, m_rows.shape, 1)
        out = jnp.where(r == c, 1.953125, 0.0) + 1.25 * y - 0.390625 * m3_rows
        out = out - 0.25 * dot(narrow(y), narrow(m3))
        return narrow(scale * out)

    m, scale = refresh_stats(1, dot(g, g, (0, 0)))
    m2 = advance(m)
    m3 = advance(m2)
    root = root_of(m, m, m2, m2, m3, m3, 0, scale)
    root = jnp.where(fresh[1] == 1, root, right[...])
    right[...] = root
    new_roots[1] = right[own, :]
    mixed = narrow(dot(g, root))

    m, scale = refresh_stats(0, dot(g, g, (1, 1)))
    work[0] = m
    m2 = advance(m)
    work[1] = m2
    m3 = advance(m2)
    work[2] = m3
    rows = root_of(m, work[0, own, :], m2, work[1, own, :], m3, work[2, own, :], quarter * ROWS, scale)
    rows = jnp.where(fresh[0] == 1, rows, left_old[...])
    new_roots[0] = rows
    update[...] = narrow(dot(rows, mixed) * math.sqrt(B))


def finish(place, fresh, decay, *arrays):
    smem = pl.BlockSpec(memory_space=pltpu.SMEM)
    vmem = pl.BlockSpec(memory_space=pltpu.VMEM)
    return pl.pallas_call(
        finish_kernel,
        name="finish",
        out_shape=(
            jax.ShapeDtypeStruct((ROWS, B), jnp.bfloat16),
            jax.ShapeDtypeStruct((2, ROWS, B), jnp.float32),
            jax.ShapeDtypeStruct((2, ROWS, B), jnp.bfloat16),
        ),
        in_specs=[smem] * 3 + [vmem] * 13,
        out_specs=(vmem,) * 3,
        scratch_shapes=[
            pltpu.VMEM((B, B), jnp.bfloat16),
            pltpu.VMEM((2, B, B), jnp.float32),
            pltpu.VMEM((B, B), jnp.bfloat16),
            pltpu.VMEM((3, B, B), jnp.float32),
        ],
        compiler_params=pltpu.CompilerParams(vmem_limit_bytes=14 << 20),
        cost_estimate=pl.CostEstimate(flops=18 * 2 * B**3, bytes_accessed=6 << 20, transcendentals=0),
    )(place, fresh, decay, *arrays)


def cut_kernel(place, cotangents, activations, *outs):
    for i, k in enumerate((2, 1, 3, 0)):
        t = lax.rem(place[0] + k, 4)
        out = outs[2 * i]
        out[:, : 2 * B] = cotangents[:, pl.ds(pl.multiple_of(t * 4 * B, 4 * B), 2 * B)]
        out[:, 2 * B :] = activations[...]
        t = lax.rem(place[1] + k, 4)
        out = outs[2 * i + 1]
        for j in range(4):
            start = pl.multiple_of(t * (B // 2) + (4 * j + 2) * B, B // 2)
            out[:, j * (B // 2) : (j + 1) * (B // 2)] = cotangents[:, pl.ds(start, B // 2)]
        out[:, 2 * B :] = activations[...]


def cut(place, cotangents, activations):
    vmem = pl.BlockSpec(memory_space=pltpu.VMEM)
    return pl.pallas_call(
        cut_kernel,
        name="cut",
        out_shape=(jax.ShapeDtypeStruct((TOKENS, WIDE), jnp.bfloat16),) * 8,
        in_specs=[pl.BlockSpec(memory_space=pltpu.SMEM), vmem, vmem],
        out_specs=(vmem,) * 8,
        compiler_params=pltpu.CompilerParams(vmem_limit_bytes=1 << 20),
        cost_estimate=pl.CostEstimate(flops=0, bytes_accessed=6 << 20, transcendentals=0),
    )(place, cotangents, activations)


def product_kernel(core, p0, p1, p2, p3, keep, send):
    parts = (p0, p1, p2, p3)
    right = jnp.concatenate([p[:, 2 * B :] for p in parts], axis=0)
    for out, side in ((send, 1 - core[0]), (keep, core[0])):
        left = jnp.concatenate(
            [
                jnp.concatenate(
                    [p[:, pl.ds(pl.multiple_of((2 * g + side) * ROWS, ROWS), ROWS)] for g in range(4)], axis=1
                )
                for p in parts
            ],
            axis=0,
        )
        out[...] = dot(left, right, (0, 0)).reshape(4, ROWS, B).astype(out.dtype)


def product(core, parts):
    vmem = pl.BlockSpec(memory_space=pltpu.VMEM)
    return pl.pallas_call(
        product_kernel,
        name="product",
        out_shape=(
            jax.ShapeDtypeStruct((4, ROWS, B), jnp.float32),
            jax.ShapeDtypeStruct((4, ROWS, B), SEND),
        ),
        in_specs=[pl.BlockSpec(memory_space=pltpu.SMEM)] + [vmem] * 4,
        out_specs=(vmem,) * 2,
        compiler_params=pltpu.CompilerParams(vmem_limit_bytes=8 << 20),
        cost_estimate=pl.CostEstimate(flops=4 * B**3, bytes_accessed=3 << 20, transcendentals=0),
    )(core, *parts)


def core_sum_kernel(place, keep, came, own, *sends):
    for k, out in zip((0, 2, 1, 3), (own,) + sends):
        t = lax.rem(place[0] + k, 4)
        out[...] = (keep[t] + came[t].astype(jnp.float32)).astype(out.dtype)


def core_sum(place, keep, came):
    vmem = pl.BlockSpec(memory_space=pltpu.VMEM)
    return pl.pallas_call(
        core_sum_kernel,
        name="core_sum",
        out_shape=(jax.ShapeDtypeStruct((ROWS, B), jnp.float32),) + (jax.ShapeDtypeStruct((ROWS, B), SEND),) * 3,
        in_specs=[pl.BlockSpec(memory_space=pltpu.SMEM)] + [vmem] * 2,
        out_specs=(vmem,) * 4,
        compiler_params=pltpu.CompilerParams(vmem_limit_bytes=1 << 20),
        cost_estimate=pl.CostEstimate(flops=4 * ROWS * B, bytes_accessed=2 << 20, transcendentals=0),
    )(place, keep, came)


def per_device(activations, cotangents, statistics, roots, ages, refresh):
    x, y = lax.axis_index(X), lax.axis_index("y")
    x_hi, x_lo, z_hi, z_lo = (lax.axis_index(a) for a in ("x_hi", "x_lo", "z_hi", "z_lo"))
    core = lax.axis_index("core")

    def scalars(*values):
        return jnp.stack(values).astype(jnp.int32)

    pieces = cut(scalars(y, x), cotangents, activations)
    y_parts, x_parts = [pieces[6]], [pieces[7]]
    for i, k in enumerate((2, 1, 3)):
        y_parts.append(shift(pieces[2 * i], "y", k))
        x_parts.append(shift(pieces[2 * i + 1], X, k))
    stats_core, right_core = partner(statistics, "core"), partner(roots[1], "core")

    y_keep, y_send = product(scalars(core), y_parts)
    y_came = partner(y_send, "core")
    x_keep, x_send = product(scalars(core), x_parts)
    x_came = partner(x_send, "core")
    y_total, *y_sends = core_sum(scalars(x), y_keep, y_came)
    x_total, *x_sends = core_sum(scalars(y), x_keep, x_came)
    for i, k in enumerate((2, 1, 3)):
        y_total += shift(y_sends[i], X, k).astype(jnp.float32)
        x_total += shift(x_sends[i], "y", k).astype(jnp.float32)

    keep = jnp.where(z_hi == 0, y_total, x_total)
    send = jnp.where(z_hi == 0, x_total, y_total).astype(SEND)
    keep, send, statistics, right = lax.optimization_barrier((keep, send, statistics, roots[1]))
    part = rounded(keep + swap_z(send, 7).astype(jnp.float32))
    stats_x, right_x = partner(statistics, "x_lo"), partner(right, "x_lo")
    part = rounded(part.astype(jnp.float32) + swap_z(part, 1).astype(jnp.float32))
    part = rounded(part.astype(jnp.float32) + swap_z(part, 2).astype(jnp.float32))
    part_x, part_core = partner(part, "x_lo"), partner(part, "core")
    grads = (part, part_x, part_core, partner(part_x, "core"))
    stats = (statistics, stats_x, stats_core, partner(stats_x, "core"))
    rights = (right, right_x, right_core, partner(right_x, "core"))

    block = y * 4 + z_hi * 2 + x_hi
    ages_here = lax.dynamic_slice_in_dim(ages, 2 * block, 2, 0)
    fresh = lax.dynamic_slice_in_dim(refresh, 2 * block, 2, 0)
    decay = decay_base ** ages_here.astype(jnp.float32)
    return finish(scalars(x_lo, core), fresh, decay, *grads, *stats, *rights, roots[0])


def solution(mesh):
    split = Mesh(mesh.devices.reshape(4, 4, 2, 2, 2, 2), EVERY)
    placed = (P(EVERY, None), P(EVERY, None), P(None, SHARD, None), P(None, SHARD, None), P(), P())
    return jax.shard_map(
        per_device,
        mesh=split,
        in_specs=placed,
        out_specs=(P(SHARD, None), P(None, SHARD, None), P(None, SHARD, None)),
        check_vma=False,
    )
```

```python
import functools
import math

import jax
import jax.numpy as jnp
from jax import lax
from jax.experimental import pallas as pl
from jax.experimental.pallas import tpu as pltpu
from jax.sharding import Mesh
from jax.sharding import PartitionSpec as P

X = ("x_hi", "x_lo")
Z = ("z_lo", "z_hi")
SHARD = ("y", "z_hi", "x_hi", "x_lo", "core")
EVERY = ("z_lo",) + SHARD

B = 512
ROWS = 128
TOKENS = 128
WIDE = 3 * B
SEND = jnp.bfloat16
VMEM = pl.BlockSpec(memory_space=pltpu.VMEM)

decay_base = 0.9
tiny_term = 1e-06


def shift(x, axis, by):
    n = lax.axis_size(axis)
    return lax.ppermute(x, axis, [(i, (i + by) % n) for i in range(n)])


def swap_z(x, bits):
    spot = [(i % 4) * 2 + i // 4 for i in range(8)]
    return lax.ppermute(x, Z, [(spot[i], spot[i ^ bits]) for i in range(8)])


def partner(x, axis, bits=1):
    n = lax.axis_size(axis)
    return lax.ppermute(x, axis, [(i, i ^ bits) for i in range(n)])


def dot(a, b, contract=(1, 0)):
    dims = (((contract[0],), (contract[1],)), ((), ()))
    return lax.dot_general(a, b, dims, preferred_element_type=jnp.float32)


def narrow(x):
    return x.astype(jnp.bfloat16)


def rounded(x):
    return lax.optimization_barrier(narrow(x))


def finish_kernel(decays, refresh, g0, g1, g2, g3, old_stats, old_right, left_old,
                  update, new_stats, new_roots, grad, full, right, work):
    at = places()
    quarter = at["x_lo"] * 2 + at["core"]
    own = quarter_rows(at, 0, 0)
    factor = 2 * (at["y"] * 4 + at["z_hi"] * 2 + at["x_hi"])
    decay = (decays[factor], decays[factor + 1])
    fresh = (refresh[factor], refresh[factor + 1])
    for a in range(2):
        for b in range(2):
            grad[quarter_rows(at, a, b), :] = (g0, g1, g2, g3)[2 * b + a][...]
    g = grad[...]

    def refresh_stats(layer, gram):
        old = old_stats[layer]
        d = decay[layer]
        a = jnp.where(fresh[layer] == 1, d * old + (1.0 - d) * gram, old)
        full[layer] = a
        new_stats[layer] = full[layer, own, :]
        total = jnp.sum(jnp.sum(a * a, axis=0, keepdims=True), axis=1, keepdims=True)
        scaling = 2.5 / jnp.sqrt(total + tiny_term)
        return scaling * a, jnp.sqrt(jnp.sqrt(scaling))

    def advance(m):
        mb = narrow(m)
        u = narrow(dot(mb, mb) * 0.0625 - 0.625 * m)
        w = dot(u, mb)
        return 2.44140625 * m + 3.125 * w + dot(u, narrow(w))

    def root_of(m, m_rows, m2, m2_rows, m3, m3_rows, row0, scale):
        y = dot(narrow(m_rows), narrow(m2)) * 0.0625 - 0.3125 * (m_rows + m2_rows)
        r = lax.broadcasted_iota(jnp.int32, m_rows.shape, 0) + row0
        c = lax.broadcasted_iota(jnp.int32, m_rows.shape, 1)
        out = jnp.where(r == c, 1.953125, 0.0) + 1.25 * y - 0.390625 * m3_rows
        out = out - 0.25 * dot(narrow(y), narrow(m3))
        return narrow(scale * out)

    m, scale = refresh_stats(1, dot(g, g, (0, 0)))
    m2 = advance(m)
    m3 = advance(m2)
    root = root_of(m, m, m2, m2, m3, m3, 0, scale)
    root = jnp.where(fresh[1] == 1, root, old_right[...])
    right[...] = root
    new_roots[1] = right[own, :]
    mixed = narrow(dot(g, root))

    m, scale = refresh_stats(0, dot(g, g, (1, 1)))
    work[0] = m
    m2 = advance(m)
    work[1] = m2
    m3 = advance(m2)
    work[2] = m3
    rows = root_of(m, work[0, own, :], m2, work[1, own, :], m3, work[2, own, :], quarter * ROWS, scale)
    rows = jnp.where(fresh[0] == 1, rows, left_old[...])
    new_roots[0] = rows
    update[...] = narrow(dot(rows, mixed) * math.sqrt(B))


def finish(decays, refresh, *arrays):
    smem = pl.BlockSpec(memory_space=pltpu.SMEM)
    return pl.pallas_call(
        finish_kernel,
        name="finish",
        out_shape=(
            jax.ShapeDtypeStruct((ROWS, B), jnp.bfloat16),
            jax.ShapeDtypeStruct((2, ROWS, B), jnp.float32),
            jax.ShapeDtypeStruct((2, ROWS, B), jnp.bfloat16),
        ),
        in_specs=[smem] * 2 + [VMEM] * 7,
        out_specs=(VMEM,) * 3,
        scratch_shapes=[
            pltpu.VMEM((B, B), jnp.bfloat16),
            pltpu.VMEM((2, B, B), jnp.float32),
            pltpu.VMEM((B, B), jnp.bfloat16),
            pltpu.VMEM((3, B, B), jnp.float32),
        ],
        compiler_params=pltpu.CompilerParams(vmem_limit_bytes=16 << 20),
        cost_estimate=pl.CostEstimate(flops=18 * 2 * B**3, bytes_accessed=6 << 20, transcendentals=0),
    )(decays, refresh, *arrays)


def places():
    return {name: lax.axis_index(name) for name in EVERY}


def cut_kernel(cotangents, activations, *rest):
    outs, sem = rest[:-1], rest[-1]
    at = places()
    copies = []

    def copy(src, dst):
        copies.append(pltpu.make_async_copy(src, dst, sem.at[len(copies)]))
        copies[-1].start()

    for i, k in enumerate((2, 1, 3, 0)):
        t = lax.rem(at["y"] + k, 4)
        copy(cotangents.at[:, pl.ds(pl.multiple_of(t * 4 * B, 4 * B), 2 * B)], outs[2 * i].at[:, : 2 * B])
        copy(activations, outs[2 * i].at[:, 2 * B :])
        t = lax.rem(at["x_hi"] * 2 + at["x_lo"] + k, 4)
        for j in range(4):
            start = pl.multiple_of(t * (B // 2) + (4 * j + 2) * B, B // 2)
            here = slice(j * (B // 2), (j + 1) * (B // 2))
            copy(cotangents.at[:, pl.ds(start, B // 2)], outs[2 * i + 1].at[:, here])
        copy(activations, outs[2 * i + 1].at[:, 2 * B :])
    for c in copies:
        c.wait()


def cut(cotangents, activations):
    free = pl.BlockSpec(memory_space=pltpu.HBM)
    return pl.pallas_call(
        cut_kernel,
        name="cut",
        out_shape=(jax.ShapeDtypeStruct((TOKENS, WIDE), jnp.bfloat16),) * 8,
        in_specs=[free, free],
        out_specs=(VMEM,) * 8,
        scratch_shapes=[pltpu.SemaphoreType.DMA((28,))],
        compiler_params=pltpu.CompilerParams(vmem_limit_bytes=4 << 20),
        cost_estimate=pl.CostEstimate(flops=0, bytes_accessed=6 << 20, transcendentals=0),
    )(cotangents, activations)


def product_kernel(p0, p1, p2, p3, keep, send):
    parts = (p0, p1, p2, p3)
    right = jnp.concatenate([p[:, 2 * B :] for p in parts], axis=0)
    core = lax.axis_index("core")
    for out, side in ((send, 1 - core), (keep, core)):
        left = jnp.concatenate(
            [
                jnp.concatenate(
                    [p[:, pl.ds(pl.multiple_of((2 * g + side) * ROWS, ROWS), ROWS)] for g in range(4)], axis=1
                )
                for p in parts
            ],
            axis=0,
        )
        out[...] = dot(left, right, (0, 0)).reshape(4, ROWS, B).astype(out.dtype)


def product(parts):
    return pl.pallas_call(
        product_kernel,
        name="product",
        out_shape=(
            jax.ShapeDtypeStruct((4, ROWS, B), jnp.float32),
            jax.ShapeDtypeStruct((4, ROWS, B), SEND),
        ),
        in_specs=[VMEM] * 4,
        out_specs=(VMEM,) * 2,
        compiler_params=pltpu.CompilerParams(vmem_limit_bytes=8 << 20),
        cost_estimate=pl.CostEstimate(flops=4 * B**3, bytes_accessed=3 << 20, transcendentals=0),
    )(*parts)


def core_sum_kernel(along_x, keep, came, own, *sends):
    at = places()
    me = at["x_hi"] * 2 + at["x_lo"] if along_x else at["y"]
    for k, out in zip((0, 2, 1, 3), (own,) + sends):
        t = lax.rem(me + k, 4)
        out[...] = (keep[t] + came[t].astype(jnp.float32)).astype(out.dtype)


def core_sum(along_x, keep, came):
    return pl.pallas_call(
        functools.partial(core_sum_kernel, along_x),
        name="core_sum",
        out_shape=(jax.ShapeDtypeStruct((ROWS, B), jnp.float32),) + (jax.ShapeDtypeStruct((ROWS, B), SEND),) * 3,
        in_specs=[VMEM] * 2,
        out_specs=(VMEM,) * 4,
        compiler_params=pltpu.CompilerParams(vmem_limit_bytes=1 << 20),
        cost_estimate=pl.CostEstimate(flops=4 * ROWS * B, bytes_accessed=2 << 20, transcendentals=0),
    )(keep, came)


def plane_sum_kernel(y0, y1, y2, y3, x0, x1, x2, x3, keep, send):
    def total(parts):
        first, second, third = (p[...].astype(jnp.float32) for p in parts[1:])
        return parts[0][...] + first + second + third

    low = lax.axis_index("z_hi") == 0

    @pl.when(low)
    def _():
        keep[...] = total((y0, y1, y2, y3))
        send[...] = total((x0, x1, x2, x3)).astype(SEND)

    @pl.when(jnp.logical_not(low))
    def _():
        keep[...] = total((x0, x1, x2, x3))
        send[...] = total((y0, y1, y2, y3)).astype(SEND)


def plane_sum(y_parts, x_parts):
    return pl.pallas_call(
        plane_sum_kernel,
        name="plane_sum",
        out_shape=(jax.ShapeDtypeStruct((ROWS, B), jnp.float32), jax.ShapeDtypeStruct((ROWS, B), SEND)),
        in_specs=[VMEM] * 8,
        out_specs=(VMEM,) * 2,
        compiler_params=pltpu.CompilerParams(vmem_limit_bytes=2 << 20),
        cost_estimate=pl.CostEstimate(flops=8 * ROWS * B, bytes_accessed=2 << 20, transcendentals=0),
    )(*y_parts, *x_parts)


def quarter_rows(at, a, b):
    top = ((at["x_lo"] ^ a) * 2 + (at["core"] ^ b)) * ROWS
    return pl.ds(pl.multiple_of(top, ROWS), ROWS)


def assemble_kernel(own, p0, p1, p2, p3, full, right):
    at = places()
    for a in range(2):
        for b in range(2):
            pack = (p0, p1, p2, p3)[2 * b + a]
            here = quarter_rows(at, a, b)
            right[here, :] = pack[2]
            for layer in range(2):
                full[layer, here, :] = pack[layer].astype(jnp.float32) if a + b else own[layer]


def assemble(own, packs):
    return pl.pallas_call(
        assemble_kernel,
        name="assemble",
        out_shape=(jax.ShapeDtypeStruct((2, B, B), jnp.float32), jax.ShapeDtypeStruct((B, B), jnp.bfloat16)),
        in_specs=[VMEM] * 5,
        out_specs=(VMEM,) * 2,
        compiler_params=pltpu.CompilerParams(vmem_limit_bytes=1 << 20),
        cost_estimate=pl.CostEstimate(flops=0, bytes_accessed=4 << 20, transcendentals=0),
    )(own, *packs)


def per_device(activations, cotangents, statistics, roots, ages, refresh):
    decays = decay_base ** ages.astype(jnp.float32)
    pieces = cut(cotangents, activations)
    y_parts, x_parts = [pieces[6]], [pieces[7]]
    for i, k in enumerate((2, 1, 3)):
        y_parts.append(shift(pieces[2 * i], "y", k))
        x_parts.append(shift(pieces[2 * i + 1], X, k))
    pack = jnp.concatenate([narrow(statistics), roots[1:]], axis=0)
    pack_core = partner(pack, "core")

    y_keep, y_send = product(y_parts)
    y_came = partner(y_send, "core")
    x_keep, x_send = product(x_parts)
    x_came = partner(x_send, "core")
    y_own, *y_sends = core_sum(True, y_keep, y_came)
    x_own, *x_sends = core_sum(False, x_keep, x_came)
    y_sums, x_sums = [y_own], [x_own]
    for i, k in enumerate((2, 1, 3)):
        y_sums.append(shift(y_sends[i], X, k))
        x_sums.append(shift(x_sends[i], "y", k))

    keep, send = plane_sum(y_sums, x_sums)
    keep, send, pack = lax.optimization_barrier((keep, send, pack))
    part = rounded(keep + swap_z(send, 7).astype(jnp.float32))
    pack_x = partner(pack, "x_lo")
    part = rounded(part.astype(jnp.float32) + swap_z(part, 1).astype(jnp.float32))
    part = rounded(part.astype(jnp.float32) + swap_z(part, 2).astype(jnp.float32))
    part_x, part_core = partner(part, "x_lo"), partner(part, "core")
    grads = (part, part_x, part_core, partner(part_x, "core"))
    full, right = assemble(statistics, (pack, pack_x, pack_core, partner(pack_x, "core")))
    return finish(decays, refresh, *grads, full, right, roots[0])


def solution(mesh):
    split = Mesh(mesh.devices.reshape(4, 4, 2, 2, 2, 2), EVERY)
    placed = (P(EVERY, None), P(EVERY, None), P(None, SHARD, None), P(None, SHARD, None), P(), P())
    return jax.shard_map(
        per_device,
        mesh=split,
        in_specs=placed,
        out_specs=(P(SHARD, None), P(None, SHARD, None), P(None, SHARD, None)),
        check_vma=False,
    )
```

```python
import functools
import math

import jax
import jax.numpy as jnp
from jax import lax
from jax.experimental import pallas as pl
from jax.experimental.pallas import tpu as pltpu
from jax.sharding import Mesh
from jax.sharding import PartitionSpec as P

X = ("x_hi", "x_lo")
Z = ("z_lo", "z_hi")
SHARD = ("y", "z_hi", "x_hi", "x_lo", "core")
EVERY = ("z_lo",) + SHARD

B = 512
ROWS = 128
TOKENS = 128
WIDE = 3 * B
SEND = jnp.bfloat16
VMEM = pl.BlockSpec(memory_space=pltpu.VMEM)

decay_base = 0.9
tiny_term = 1e-06


def shift(x, axis, by):
    n = lax.axis_size(axis)
    return lax.ppermute(x, axis, [(i, (i + by) % n) for i in range(n)])


def swap_z(x, bits):
    spot = [(i % 4) * 2 + i // 4 for i in range(8)]
    return lax.ppermute(x, Z, [(spot[i], spot[i ^ bits]) for i in range(8)])


def partner(x, axis, bits=1):
    n = lax.axis_size(axis)
    return lax.ppermute(x, axis, [(i, i ^ bits) for i in range(n)])


def dot(a, b, contract=(1, 0)):
    dims = (((contract[0],), (contract[1],)), ((), ()))
    return lax.dot_general(a, b, dims, preferred_element_type=jnp.float32)


def narrow(x):
    return x.astype(jnp.bfloat16)


def rounded(x):
    return lax.optimization_barrier(narrow(x))


def finish_kernel(decays, refresh, g0, g1, g2, g3, old_stats, old_right, left_old,
                  update, new_stats, new_roots, grad, full, right, work):
    at = places()
    quarter = at["x_lo"] * 2 + at["core"]
    own = quarter_rows(at, 0, 0)
    factor = 2 * (at["y"] * 4 + at["z_hi"] * 2 + at["x_hi"])
    decay = (decays[factor], decays[factor + 1])
    fresh = (refresh[factor], refresh[factor + 1])
    for a in range(2):
        for b in range(2):
            grad[quarter_rows(at, a, b), :] = (g0, g1, g2, g3)[2 * b + a][...]
    g = grad[...]

    def refresh_stats(layer, gram):
        old = old_stats[layer]
        d = decay[layer]
        a = jnp.where(fresh[layer] == 1, d * old + (1.0 - d) * gram, old)
        full[layer] = a
        new_stats[layer] = full[layer, own, :]
        total = jnp.sum(jnp.sum(a * a, axis=0, keepdims=True), axis=1, keepdims=True)
        scaling = 2.5 / jnp.sqrt(total + tiny_term)
        return scaling * a, jnp.sqrt(jnp.sqrt(scaling))

    def both(f, *pairs):
        return f(*(p[0] for p in pairs)), f(*(p[1] for p in pairs))

    def advance(m):
        mb = both(narrow, m)
        square = both(dot, mb, mb)
        u = both(lambda s, v: narrow(s * 0.0625 - 0.625 * v), square, m)
        w = both(dot, u, mb)
        wb = both(narrow, w)
        last = both(dot, u, wb)
        return both(lambda v, w, t: 2.44140625 * v + 3.125 * w + t, m, w, last), mb

    def spread(shape, row0):
        r = lax.broadcasted_iota(jnp.int32, shape, 0) + row0
        c = lax.broadcasted_iota(jnp.int32, shape, 1)
        return jnp.where(r == c, 1.953125, 0.0)

    grams = (dot(g, g, (1, 1)), dot(g, g, (0, 0)))
    m, scale = zip(refresh_stats(0, grams[0]), refresh_stats(1, grams[1]))
    work[0] = m[0]
    m2, mb = advance(m)
    work[1] = m2[0]
    m3, m2b = advance(m2)
    work[2] = m3[0]
    m3b = both(narrow, m3)
    rows = [work[i, own, :] for i in range(3)]
    first = (rows[0], m[1]), (rows[1], m2[1]), (rows[2], m3[1])
    product = dot(narrow(rows[0]), m2b[0]), dot(mb[1], m2b[1])
    y = both(lambda p, v, v2: p * 0.0625 - 0.3125 * (v + v2), product, first[0], first[1])
    product = both(dot, both(narrow, y), m3b)
    diagonal = spread((ROWS, B), quarter * ROWS), spread((B, B), 0)
    out = both(
        lambda e, v, v3, p, s: narrow(s * (e + 1.25 * v - 0.390625 * v3 - 0.25 * p)),
        diagonal, y, first[2], product, scale,
    )
    root = jnp.where(fresh[1] == 1, out[1], old_right[...])
    mixed = narrow(dot(g, root))
    right[...] = root
    new_roots[1] = right[own, :]
    left = jnp.where(fresh[0] == 1, out[0], left_old[...])
    new_roots[0] = left
    update[...] = narrow(dot(left, mixed) * math.sqrt(B))


def finish(decays, refresh, *arrays):
    smem = pl.BlockSpec(memory_space=pltpu.SMEM)
    return pl.pallas_call(
        finish_kernel,
        name="finish",
        out_shape=(
            jax.ShapeDtypeStruct((ROWS, B), jnp.bfloat16),
            jax.ShapeDtypeStruct((2, ROWS, B), jnp.float32),
            jax.ShapeDtypeStruct((2, ROWS, B), jnp.bfloat16),
        ),
        in_specs=[smem] * 2 + [VMEM] * 7,
        out_specs=(VMEM,) * 3,
        scratch_shapes=[
            pltpu.VMEM((B, B), jnp.bfloat16),
            pltpu.VMEM((2, B, B), jnp.float32),
            pltpu.VMEM((B, B), jnp.bfloat16),
            pltpu.VMEM((3, B, B), jnp.float32),
        ],
        compiler_params=pltpu.CompilerParams(vmem_limit_bytes=16 << 20),
        cost_estimate=pl.CostEstimate(flops=18 * 2 * B**3, bytes_accessed=6 << 20, transcendentals=0),
    )(decays, refresh, *arrays)


def places():
    return {name: lax.axis_index(name) for name in EVERY}


def cut_kernel(cotangents, activations, *rest):
    outs, held, sem = rest[:-2], rest[-2], rest[-1]
    at = places()
    copies = []

    def copy(src, dst):
        copies.append(pltpu.make_async_copy(src, dst, sem.at[len(copies)]))
        copies[-1].start()

    copy(activations, held)
    for i, k in enumerate((2, 1, 3, 0)):
        t = lax.rem(at["y"] + k, 4)
        copy(cotangents.at[:, pl.ds(pl.multiple_of(t * 4 * B, 4 * B), 2 * B)], outs[2 * i].at[:, : 2 * B])
        t = lax.rem(at["x_hi"] * 2 + at["x_lo"] + k, 4)
        for j in range(4):
            start = pl.multiple_of(t * (B // 2) + (4 * j + 2) * B, B // 2)
            here = slice(j * (B // 2), (j + 1) * (B // 2))
            copy(cotangents.at[:, pl.ds(start, B // 2)], outs[2 * i + 1].at[:, here])
    copies[0].wait()
    for out in outs:
        out[:, 2 * B :] = held[...]
    for c in copies[1:]:
        c.wait()


def cut(cotangents, activations):
    free = pl.BlockSpec(memory_space=pltpu.HBM)
    cotangents = pltpu.with_memory_space_constraint(cotangents, pltpu.HBM)
    activations = pltpu.with_memory_space_constraint(activations, pltpu.HBM)
    return pl.pallas_call(
        cut_kernel,
        name="cut",
        out_shape=(jax.ShapeDtypeStruct((TOKENS, WIDE), jnp.bfloat16),) * 8,
        in_specs=[free, free],
        out_specs=(VMEM,) * 8,
        scratch_shapes=[pltpu.VMEM((TOKENS, B), jnp.bfloat16), pltpu.SemaphoreType.DMA((21,))],
        compiler_params=pltpu.CompilerParams(vmem_limit_bytes=4 << 20),
        cost_estimate=pl.CostEstimate(flops=0, bytes_accessed=6 << 20, transcendentals=0),
    )(cotangents, activations)


def product_kernel(p0, p1, p2, p3, keep, send):
    parts = (p0, p1, p2, p3)
    right = jnp.concatenate([p[:, 2 * B :] for p in parts], axis=0)
    core = lax.axis_index("core")
    for out, side in ((send, 1 - core), (keep, core)):
        left = jnp.concatenate(
            [
                jnp.concatenate(
                    [p[:, pl.ds(pl.multiple_of((2 * g + side) * ROWS, ROWS), ROWS)] for g in range(4)], axis=1
                )
                for p in parts
            ],
            axis=0,
        )
        out[...] = dot(left, right, (0, 0)).reshape(4, ROWS, B).astype(out.dtype)


def product(parts):
    return pl.pallas_call(
        product_kernel,
        name="product",
        out_shape=(
            jax.ShapeDtypeStruct((4, ROWS, B), jnp.float32),
            jax.ShapeDtypeStruct((4, ROWS, B), SEND),
        ),
        in_specs=[VMEM] * 4,
        out_specs=(VMEM,) * 2,
        compiler_params=pltpu.CompilerParams(vmem_limit_bytes=8 << 20),
        cost_estimate=pl.CostEstimate(flops=4 * B**3, bytes_accessed=3 << 20, transcendentals=0),
    )(*parts)


def core_sum_kernel(along_x, keep, came, own, *sends):
    at = places()
    me = at["x_hi"] * 2 + at["x_lo"] if along_x else at["y"]
    for k, out in zip((0, 2, 1, 3), (own,) + sends):
        t = lax.rem(me + k, 4)
        out[...] = (keep[t] + came[t].astype(jnp.float32)).astype(out.dtype)


def core_sum(along_x, keep, came):
    return pl.pallas_call(
        functools.partial(core_sum_kernel, along_x),
        name="core_sum",
        out_shape=(jax.ShapeDtypeStruct((ROWS, B), jnp.float32),) + (jax.ShapeDtypeStruct((ROWS, B), SEND),) * 3,
        in_specs=[VMEM] * 2,
        out_specs=(VMEM,) * 4,
        compiler_params=pltpu.CompilerParams(vmem_limit_bytes=1 << 20),
        cost_estimate=pl.CostEstimate(flops=4 * ROWS * B, bytes_accessed=2 << 20, transcendentals=0),
    )(keep, came)


def plane_sum_kernel(y0, y1, y2, y3, x0, x1, x2, x3, keep, send):
    def total(parts):
        first, second, third = (p[...].astype(jnp.float32) for p in parts[1:])
        return parts[0][...] + first + second + third

    low = lax.axis_index("z_hi") == 0

    @pl.when(low)
    def _():
        keep[...] = total((y0, y1, y2, y3))
        send[...] = total((x0, x1, x2, x3)).astype(SEND)

    @pl.when(jnp.logical_not(low))
    def _():
        keep[...] = total((x0, x1, x2, x3))
        send[...] = total((y0, y1, y2, y3)).astype(SEND)


def plane_sum(y_parts, x_parts):
    return pl.pallas_call(
        plane_sum_kernel,
        name="plane_sum",
        out_shape=(jax.ShapeDtypeStruct((ROWS, B), jnp.float32), jax.ShapeDtypeStruct((ROWS, B), SEND)),
        in_specs=[VMEM] * 8,
        out_specs=(VMEM,) * 2,
        compiler_params=pltpu.CompilerParams(vmem_limit_bytes=2 << 20),
        cost_estimate=pl.CostEstimate(flops=8 * ROWS * B, bytes_accessed=2 << 20, transcendentals=0),
    )(*y_parts, *x_parts)


def quarter_rows(at, a, b):
    top = ((at["x_lo"] ^ a) * 2 + (at["core"] ^ b)) * ROWS
    return pl.ds(pl.multiple_of(top, ROWS), ROWS)


def assemble_kernel(own, p0, p1, p2, p3, full, right):
    at = places()
    for a in range(2):
        for b in range(2):
            pack = (p0, p1, p2, p3)[2 * b + a]
            here = quarter_rows(at, a, b)
            right[here, :] = pack[2]
            for layer in range(2):
                full[layer, here, :] = pack[layer].astype(jnp.float32) if a + b else own[layer]


def assemble(own, packs):
    return pl.pallas_call(
        assemble_kernel,
        name="assemble",
        out_shape=(jax.ShapeDtypeStruct((2, B, B), jnp.float32), jax.ShapeDtypeStruct((B, B), jnp.bfloat16)),
        in_specs=[VMEM] * 5,
        out_specs=(VMEM,) * 2,
        compiler_params=pltpu.CompilerParams(vmem_limit_bytes=1 << 20),
        cost_estimate=pl.CostEstimate(flops=0, bytes_accessed=4 << 20, transcendentals=0),
    )(own, *packs)


def per_device(activations, cotangents, statistics, roots, ages, refresh):
    decays = decay_base ** ages.astype(jnp.float32)
    pieces = cut(cotangents, activations)
    y_parts, x_parts = [pieces[6]], [pieces[7]]
    for i, k in enumerate((2, 1, 3)):
        y_parts.append(shift(pieces[2 * i], "y", k))
        x_parts.append(shift(pieces[2 * i + 1], X, k))

    y_keep, y_send = product(y_parts)
    y_came = partner(y_send, "core")
    x_keep, x_send = product(x_parts)
    x_came = partner(x_send, "core")
    y_own, *y_sends = core_sum(True, y_keep, y_came)
    x_own, *x_sends = core_sum(False, x_keep, x_came)
    y_sums, x_sums = [y_own], [x_own]
    for i, k in enumerate((2, 1, 3)):
        y_sums.append(shift(y_sends[i], X, k))
        x_sums.append(shift(x_sends[i], "y", k))

    keep, send = plane_sum(y_sums, x_sums)
    pack = jnp.concatenate([narrow(statistics), roots[1:]], axis=0)
    keep, send, pack = lax.optimization_barrier((keep, send, pack))
    part = rounded(keep + swap_z(send, 7).astype(jnp.float32))
    pack_x = partner(pack, "x_lo")
    part, pack_core = lax.optimization_barrier((part, partner(pack, "core")))
    part = rounded(part.astype(jnp.float32) + swap_z(part, 1).astype(jnp.float32))
    part, pack_x = lax.optimization_barrier((part, pack_x))
    part = rounded(part.astype(jnp.float32) + swap_z(part, 2).astype(jnp.float32))
    part_x, part_core = partner(part, "x_lo"), partner(part, "core")
    grads = (part, part_x, part_core, partner(part_x, "core"))
    full, right = assemble(statistics, (pack, pack_x, pack_core, partner(pack_x, "core")))
    return finish(decays, refresh, *grads, full, right, roots[0])


def solution(mesh):
    split = Mesh(mesh.devices.reshape(4, 4, 2, 2, 2, 2), EVERY)
    placed = (P(EVERY, None), P(EVERY, None), P(None, SHARD, None), P(None, SHARD, None), P(), P())
    return jax.shard_map(
        per_device,
        mesh=split,
        in_specs=placed,
        out_specs=(P(SHARD, None), P(None, SHARD, None), P(None, SHARD, None)),
        check_vma=False,
    )
```

```python
import functools
import math

import jax
import jax.numpy as jnp
from jax import lax
from jax.experimental import pallas as pl
from jax.experimental.pallas import tpu as pltpu
from jax.sharding import Mesh
from jax.sharding import PartitionSpec as P

X = ("x_hi", "x_lo")
Z = ("z_lo", "z_hi")
SHARD = ("y", "z_hi", "x_hi", "x_lo", "core")
EVERY = ("z_lo",) + SHARD

B = 512
ROWS = 128
TOKENS = 128
HALF = B // 2
ORDER = (2, 1, 3, 0)
WIDE = 3 * B
SEND = jnp.bfloat16
VMEM = pl.BlockSpec(memory_space=pltpu.VMEM)

decay_base = 0.9
tiny_term = 1e-06


def shift(x, along_y, by):
    pairs = []
    for y in range(4):
        for x_at in range(4):
            for core in range(2):
                moves_y = (core == 0) == along_y
                to = ((y + by) % 4, x_at) if moves_y else (y, (x_at + by) % 4)
                pairs.append(((y * 4 + x_at) * 2 + core, (to[0] * 4 + to[1]) * 2 + core))
    return lax.ppermute(x, ("y",) + X + ("core",), pairs)


def ring_spot(z, core=None):
    spot = (z % 4) * 2 + z // 4
    return spot if core is None else spot * 2 + core


def swap_z(x, bits):
    return lax.ppermute(x, Z, [(ring_spot(z), ring_spot(z ^ bits)) for z in range(8)])


def mirror(near, far):
    first, second = [], []
    for z in range(8):
        stays = z // 4
        first.append((ring_spot(z, stays), ring_spot(z, 1 - stays)))
        first.append((ring_spot(z, 1 - stays), ring_spot(7 - z, 1 - stays)))
        second.append((ring_spot(z, 1 - stays), ring_spot(7 - z, stays)))
    axes = Z + ("core",)
    return lax.ppermute(near, axes, first), lax.ppermute(far, axes, second)


def partner(x, axis, bits=1):
    n = lax.axis_size(axis)
    return lax.ppermute(x, axis, [(i, i ^ bits) for i in range(n)])


def dot(a, b, contract=(1, 0)):
    dims = (((contract[0],), (contract[1],)), ((), ()))
    return lax.dot_general(a, b, dims, preferred_element_type=jnp.float32)


def narrow(x):
    return x.astype(jnp.bfloat16)


def rounded(x):
    return lax.optimization_barrier(narrow(x))


def finish_kernel(decays, refresh, g0, g1, g2, g3, old_stats, old_right, left_old,
                  update, new_stats, new_roots, grad, full, right, work):
    at = places()
    quarter = at["x_lo"] * 2 + at["core"]
    own = quarter_rows(at, 0, 0)
    factor = 2 * (at["y"] * 4 + at["z_hi"] * 2 + at["x_hi"])
    decay = (decays[factor], decays[factor + 1])
    fresh = (refresh[factor], refresh[factor + 1])
    for a in range(2):
        for b in range(2):
            grad[quarter_rows(at, a, b), :] = (g0, g1, g2, g3)[2 * b + a][...]
    g = grad[...]

    def refresh_stats(layer, gram):
        old = old_stats[layer]
        d = decay[layer]
        a = jnp.where(fresh[layer] == 1, d * old + (1.0 - d) * gram, old)
        full[layer] = a
        new_stats[layer] = full[layer, own, :]
        total = jnp.sum(jnp.sum(a * a, axis=0, keepdims=True), axis=1, keepdims=True)
        scaling = 2.5 / jnp.sqrt(total + tiny_term)
        return scaling * a, jnp.sqrt(jnp.sqrt(scaling))

    def both(f, *pairs):
        return f(*(p[0] for p in pairs)), f(*(p[1] for p in pairs))

    def advance(m):
        mb = both(narrow, m)
        square = both(dot, mb, mb)
        u = both(lambda s, v: narrow(s * 0.0625 - 0.625 * v), square, m)
        w = both(dot, u, mb)
        wb = both(narrow, w)
        last = both(dot, u, wb)
        return both(lambda v, w, t: 2.44140625 * v + 3.125 * w + t, m, w, last), mb

    def spread(shape, row0):
        r = lax.broadcasted_iota(jnp.int32, shape, 0) + row0
        c = lax.broadcasted_iota(jnp.int32, shape, 1)
        return jnp.where(r == c, 1.953125, 0.0)

    grams = (dot(g, g, (1, 1)), dot(g, g, (0, 0)))
    m, scale = zip(refresh_stats(0, grams[0]), refresh_stats(1, grams[1]))
    work[0] = m[0]
    m2, mb = advance(m)
    work[1] = m2[0]
    m3, m2b = advance(m2)
    work[2] = m3[0]
    m3b = both(narrow, m3)
    rows = [work[i, own, :] for i in range(3)]
    first = (rows[0], m[1]), (rows[1], m2[1]), (rows[2], m3[1])
    product = dot(narrow(rows[0]), m2b[0]), dot(mb[1], m2b[1])
    y = both(lambda p, v, v2: p * 0.0625 - 0.3125 * (v + v2), product, first[0], first[1])
    product = both(dot, both(narrow, y), m3b)
    diagonal = spread((ROWS, B), quarter * ROWS), spread((B, B), 0)
    out = both(
        lambda e, v, v3, p, s: narrow(s * (e + 1.25 * v - 0.390625 * v3 - 0.25 * p)),
        diagonal, y, first[2], product, scale,
    )
    root = jnp.where(fresh[1] == 1, out[1], old_right[...])
    mixed = narrow(dot(g, root))
    right[...] = root
    new_roots[1] = right[own, :]
    left = jnp.where(fresh[0] == 1, out[0], left_old[...])
    new_roots[0] = left
    update[...] = narrow(dot(left, mixed) * math.sqrt(B))


def finish(decays, refresh, *arrays):
    smem = pl.BlockSpec(memory_space=pltpu.SMEM)
    return pl.pallas_call(
        finish_kernel,
        name="finish",
        out_shape=(
            jax.ShapeDtypeStruct((ROWS, B), jnp.bfloat16),
            jax.ShapeDtypeStruct((2, ROWS, B), jnp.float32),
            jax.ShapeDtypeStruct((2, ROWS, B), jnp.bfloat16),
        ),
        in_specs=[smem] * 2 + [VMEM] * 7,
        out_specs=(VMEM,) * 3,
        scratch_shapes=[
            pltpu.VMEM((B, B), jnp.bfloat16),
            pltpu.VMEM((2, B, B), jnp.float32),
            pltpu.VMEM((B, B), jnp.bfloat16),
            pltpu.VMEM((3, B, B), jnp.float32),
        ],
        compiler_params=pltpu.CompilerParams(vmem_limit_bytes=16 << 20),
        cost_estimate=pl.CostEstimate(flops=18 * 2 * B**3, bytes_accessed=6 << 20, transcendentals=0),
    )(decays, refresh, *arrays)


def places():
    return {name: lax.axis_index(name) for name in EVERY}


def cut_kernel(cotangents, activations, *rest):
    outs, other, held, sem = rest[:4], rest[4], rest[5], rest[6]
    at = places()
    spot = (at["y"], at["x_hi"] * 2 + at["x_lo"])
    copies = []

    def copy(src, dst):
        copies.append(pltpu.make_async_copy(src, dst, sem.at[len(copies)]))
        copies[-1].start()

    copy(activations, held)
    pieces = [(at["core"], out) for out in outs] + [(1 - at["core"], other.at[i]) for i in range(4)]
    for (core, out), k in zip(pieces, ORDER * 2):
        for j in range(4):
            start = jnp.where(
                core == 0,
                lax.rem(spot[0] + k, 4) * (4 * B) + j * HALF,
                lax.rem(spot[1] + k, 4) * HALF + (4 * j + 2) * B,
            )
            columns = pl.ds(pl.multiple_of(start, HALF), HALF)
            copy(cotangents.at[:, columns], out.at[:, j * HALF : (j + 1) * HALF])
    copies[0].wait()
    for core, out in pieces:
        out[:, 2 * B :] = held[...]
    for c in copies[1:]:
        c.wait()


def cut(cotangents, activations):
    free = pl.BlockSpec(memory_space=pltpu.HBM)
    cotangents = pltpu.with_memory_space_constraint(cotangents, pltpu.HBM)
    activations = pltpu.with_memory_space_constraint(activations, pltpu.HBM)
    return pl.pallas_call(
        cut_kernel,
        name="cut",
        out_shape=(jax.ShapeDtypeStruct((TOKENS, WIDE), jnp.bfloat16),) * 4
        + (jax.ShapeDtypeStruct((4, TOKENS, WIDE), jnp.bfloat16),),
        in_specs=[free, free],
        out_specs=(VMEM,) * 5,
        scratch_shapes=[pltpu.VMEM((TOKENS, B), jnp.bfloat16), pltpu.SemaphoreType.DMA((33,))],
        compiler_params=pltpu.CompilerParams(vmem_limit_bytes=4 << 20),
        cost_estimate=pl.CostEstimate(flops=0, bytes_accessed=6 << 20, transcendentals=0),
    )(cotangents, activations)


def split_kernel(pieces, *outs):
    for i, out in enumerate(outs):
        out[...] = pieces[i]


def split(pieces):
    return pl.pallas_call(
        split_kernel,
        name="split",
        out_shape=(jax.ShapeDtypeStruct((TOKENS, WIDE), jnp.bfloat16),) * 4,
        in_specs=[VMEM],
        out_specs=(VMEM,) * 4,
        compiler_params=pltpu.CompilerParams(vmem_limit_bytes=1 << 20),
        cost_estimate=pl.CostEstimate(flops=0, bytes_accessed=3 << 20, transcendentals=0),
    )(pieces)


def product_kernel(*refs):
    parts, outs = refs[:8], refs[8:]
    at = places()
    me = jnp.where(at["core"] == 0, at["x_hi"] * 2 + at["x_lo"], at["y"])
    right = jnp.concatenate([p[:, 2 * B :] for p in parts], axis=0)
    for k, out in zip(ORDER, outs):
        columns = pl.ds(pl.multiple_of(lax.rem(me + k, 4) * HALF, HALF), HALF)
        left = jnp.concatenate([p[:, columns] for p in parts], axis=0)
        out[...] = dot(left, right, (0, 0)).astype(out.dtype)


def product(parts):
    return pl.pallas_call(
        product_kernel,
        name="product",
        out_shape=(jax.ShapeDtypeStruct((HALF, B), SEND),) * 3 + (jax.ShapeDtypeStruct((HALF, B), jnp.float32),),
        in_specs=[VMEM] * 8,
        out_specs=(VMEM,) * 4,
        compiler_params=pltpu.CompilerParams(vmem_limit_bytes=8 << 20),
        cost_estimate=pl.CostEstimate(flops=8 * B**3, bytes_accessed=5 << 20, transcendentals=0),
    )(*parts)


def plane_sum_kernel(first, second, third, own, keep, near, far):
    total = own[...]
    for part in (first, second, third):
        total += part[...].astype(jnp.float32)
    core = lax.axis_index("core")
    stays = core == lax.axis_index("z_hi")

    @pl.when(core == 0)
    def _():
        keep[...] = total[:ROWS]
        far[...] = total[ROWS:].astype(SEND)

    @pl.when(core == 1)
    def _():
        keep[...] = total[ROWS:]
        far[...] = total[:ROWS].astype(SEND)

    @pl.when(stays)
    def _():
        near[...] = far[...]

    @pl.when(jnp.logical_not(stays))
    def _():
        near[...] = keep[...].astype(SEND)


def plane_sum(parts):
    return pl.pallas_call(
        plane_sum_kernel,
        name="plane_sum",
        out_shape=(
            jax.ShapeDtypeStruct((ROWS, B), jnp.float32),
            jax.ShapeDtypeStruct((ROWS, B), SEND),
            jax.ShapeDtypeStruct((ROWS, B), SEND),
        ),
        in_specs=[VMEM] * 4,
        out_specs=(VMEM,) * 3,
        compiler_params=pltpu.CompilerParams(vmem_limit_bytes=2 << 20),
        cost_estimate=pl.CostEstimate(flops=8 * ROWS * B, bytes_accessed=2 << 20, transcendentals=0),
    )(*parts)


def mirror_sum_kernel(keep, near, far, out):
    stays = lax.axis_index("core") == lax.axis_index("z_hi")

    @pl.when(stays)
    def _():
        out[...] = narrow(keep[...] + near[...].astype(jnp.float32))

    @pl.when(jnp.logical_not(stays))
    def _():
        out[...] = narrow(far[...].astype(jnp.float32) + near[...].astype(jnp.float32))


def mirror_sum(keep, near, far):
    return pl.pallas_call(
        mirror_sum_kernel,
        name="mirror_sum",
        out_shape=jax.ShapeDtypeStruct((ROWS, B), jnp.bfloat16),
        in_specs=[VMEM] * 3,
        out_specs=VMEM,
        compiler_params=pltpu.CompilerParams(vmem_limit_bytes=1 << 20),
        cost_estimate=pl.CostEstimate(flops=2 * ROWS * B, bytes_accessed=1 << 19, transcendentals=0),
    )(keep, near, far)


def quarter_rows(at, a, b):
    top = ((at["x_lo"] ^ a) * 2 + (at["core"] ^ b)) * ROWS
    return pl.ds(pl.multiple_of(top, ROWS), ROWS)


def assemble_kernel(own, p0, p1, p2, p3, full, right):
    at = places()
    for a in range(2):
        for b in range(2):
            pack = (p0, p1, p2, p3)[2 * b + a]
            here = quarter_rows(at, a, b)
            right[here, :] = pack[2]
            for layer in range(2):
                full[layer, here, :] = pack[layer].astype(jnp.float32) if a + b else own[layer]


def assemble(own, packs):
    return pl.pallas_call(
        assemble_kernel,
        name="assemble",
        out_shape=(jax.ShapeDtypeStruct((2, B, B), jnp.float32), jax.ShapeDtypeStruct((B, B), jnp.bfloat16)),
        in_specs=[VMEM] * 5,
        out_specs=(VMEM,) * 2,
        compiler_params=pltpu.CompilerParams(vmem_limit_bytes=1 << 20),
        cost_estimate=pl.CostEstimate(flops=0, bytes_accessed=4 << 20, transcendentals=0),
    )(own, *packs)


def per_device(activations, cotangents, statistics, roots, ages, refresh):
    decays = decay_base ** ages.astype(jnp.float32)
    *pieces, other = cut(cotangents, activations)
    parts = [pieces[3]] + [shift(pieces[i], True, ORDER[i]) for i in range(3)]
    pieces = split(partner(other, "core"))
    parts += [pieces[3]] + [shift(pieces[i], True, ORDER[i]) for i in range(3)]

    *sends, own = product(parts)
    keep, near, far = plane_sum([shift(sends[i], False, ORDER[i]) for i in range(3)] + [own])
    pack = jnp.concatenate([narrow(statistics), roots[1:]], axis=0)
    keep, near, far, pack = lax.optimization_barrier((keep, near, far, pack))
    part = mirror_sum(keep, *mirror(near, far))
    pack_x = partner(pack, "x_lo")
    part, pack_core = lax.optimization_barrier((part, partner(pack, "core")))
    part = rounded(part.astype(jnp.float32) + swap_z(part, 1).astype(jnp.float32))
    part, pack_x = lax.optimization_barrier((part, pack_x))
    part = rounded(part.astype(jnp.float32) + swap_z(part, 2).astype(jnp.float32))
    part_x, part_core = partner(part, "x_lo"), partner(part, "core")
    grads = (part, part_x, part_core, partner(part_x, "core"))
    full, right = assemble(statistics, (pack, pack_x, pack_core, partner(pack_x, "core")))
    return finish(decays, refresh, *grads, full, right, roots[0])


def solution(mesh):
    split = Mesh(mesh.devices.reshape(4, 4, 2, 2, 2, 2), EVERY)
    placed = (P(EVERY, None), P(EVERY, None), P(None, SHARD, None), P(None, SHARD, None), P(), P())
    return jax.shard_map(
        per_device,
        mesh=split,
        in_specs=placed,
        out_specs=(P(SHARD, None), P(None, SHARD, None), P(None, SHARD, None)),
        check_vma=False,
    )
```

```python
import functools
import math

import jax
import jax.numpy as jnp
from jax import lax
from jax.experimental import pallas as pl
from jax.experimental.pallas import tpu as pltpu
from jax.sharding import Mesh
from jax.sharding import PartitionSpec as P

X = ("x_hi", "x_lo")
Z = ("z_lo", "z_hi")
SHARD = ("y", "z_hi", "x_hi", "x_lo", "core")
EVERY = ("z_lo",) + SHARD

B = 512
ROWS = 128
TOKENS = 128
HALF = B // 2
ORDER = (2, 1, 3, 0)
WIDE = 3 * B
SEND = jnp.bfloat16
VMEM = pl.BlockSpec(memory_space=pltpu.VMEM)

decay_base = 0.9
tiny_term = 1e-06


def shift(x, along_y, by):
    pairs = []
    for y in range(4):
        for x_at in range(4):
            for core in range(2):
                moves_y = (core == 0) == along_y
                to = ((y + by) % 4, x_at) if moves_y else (y, (x_at + by) % 4)
                pairs.append(((y * 4 + x_at) * 2 + core, (to[0] * 4 + to[1]) * 2 + core))
    return lax.ppermute(x, ("y",) + X + ("core",), pairs)


def ring_spot(z, core=None):
    spot = (z % 4) * 2 + z // 4
    return spot if core is None else spot * 2 + core


def swap_z(x, bits):
    return lax.ppermute(x, Z, [(ring_spot(z), ring_spot(z ^ bits)) for z in range(8)])


def mirror(near, far):
    first, second = [], []
    for z in range(8):
        stays = z // 4
        first.append((ring_spot(z, stays), ring_spot(z, 1 - stays)))
        first.append((ring_spot(z, 1 - stays), ring_spot(7 - z, 1 - stays)))
        second.append((ring_spot(z, 1 - stays), ring_spot(7 - z, stays)))
    axes = Z + ("core",)
    return lax.ppermute(near, axes, first), lax.ppermute(far, axes, second)


def partner(x, axis, bits=1):
    n = lax.axis_size(axis)
    return lax.ppermute(x, axis, [(i, i ^ bits) for i in range(n)])


def dot(a, b, contract=(1, 0)):
    dims = (((contract[0],), (contract[1],)), ((), ()))
    return lax.dot_general(a, b, dims, preferred_element_type=jnp.float32)


def narrow(x):
    return x.astype(jnp.bfloat16)


def rounded(x):
    return lax.optimization_barrier(narrow(x))


def finish_kernel(decays, refresh, g0, g1, g2, g3, old_stats, old_right, left_old,
                  update, new_stats, new_roots, grad, full, right, left, result, work, sem):
    at = places()
    quarter = at["x_lo"] * 2 + at["core"]
    own = quarter_rows(at, 0, 0)
    factor = 2 * (at["y"] * 4 + at["z_hi"] * 2 + at["x_hi"])
    decay = (decays[factor], decays[factor + 1])
    fresh = (refresh[factor], refresh[factor + 1])
    for a in range(2):
        for b in range(2):
            grad[quarter_rows(at, a, b), :] = (g0, g1, g2, g3)[2 * b + a][...]
    g = grad[...]
    writes = []

    def write(i, src, dst):
        writes.append(pltpu.make_async_copy(src, dst, sem.at[i]))
        writes[-1].start()

    def refresh_stats(layer, gram):
        old = old_stats[layer]
        d = decay[layer]
        a = jnp.where(fresh[layer] == 1, d * old + (1.0 - d) * gram, old)
        full[layer] = a
        write(layer, full.at[layer, own, :], new_stats.at[layer])
        total = jnp.sum(jnp.sum(a * a, axis=0, keepdims=True), axis=1, keepdims=True)
        scaling = 2.5 / jnp.sqrt(total + tiny_term)
        return scaling * a, jnp.sqrt(jnp.sqrt(scaling))

    def both(f, *pairs):
        return f(*(p[0] for p in pairs)), f(*(p[1] for p in pairs))

    def advance(m):
        mb = both(narrow, m)
        square = both(dot, mb, mb)
        u = both(lambda s, v: narrow(s * 0.0625 - 0.625 * v), square, m)
        w = both(dot, u, mb)
        wb = both(narrow, w)
        last = both(dot, u, wb)
        return both(lambda v, w, t: 2.44140625 * v + 3.125 * w + t, m, w, last), mb

    def spread(shape, row0):
        r = lax.broadcasted_iota(jnp.int32, shape, 0) + row0
        c = lax.broadcasted_iota(jnp.int32, shape, 1)
        return jnp.where(r == c, 1.953125, 0.0)

    grams = (dot(g, g, (1, 1)), dot(g, g, (0, 0)))
    m, scale = zip(refresh_stats(0, grams[0]), refresh_stats(1, grams[1]))
    work[0] = m[0]
    m2, mb = advance(m)
    work[1] = m2[0]
    m3, m2b = advance(m2)
    work[2] = m3[0]
    m3b = both(narrow, m3)
    rows = [work[i, own, :] for i in range(3)]
    first = (rows[0], m[1]), (rows[1], m2[1]), (rows[2], m3[1])
    product = dot(narrow(rows[0]), m2b[0]), dot(mb[1], m2b[1])
    y = both(lambda p, v, v2: p * 0.0625 - 0.3125 * (v + v2), product, first[0], first[1])
    product = both(dot, both(narrow, y), m3b)
    diagonal = spread((ROWS, B), quarter * ROWS), spread((B, B), 0)
    out = both(
        lambda e, v, v3, p, s: narrow(s * (e + 1.25 * v - 0.390625 * v3 - 0.25 * p)),
        diagonal, y, first[2], product, scale,
    )
    left[...] = jnp.where(fresh[0] == 1, out[0], left_old[...])
    write(2, left, new_roots.at[0])
    right[...] = jnp.where(fresh[1] == 1, out[1], old_right[...])
    write(3, right.at[own, :], new_roots.at[1])
    mixed = narrow(dot(g, right[...]))
    result[...] = narrow(dot(left[...], mixed) * math.sqrt(B))
    write(4, result, update)
    for w in writes:
        w.wait()


def finish(decays, refresh, *arrays):
    smem = pl.BlockSpec(memory_space=pltpu.SMEM)
    return pl.pallas_call(
        finish_kernel,
        name="finish",
        out_shape=(
            jax.ShapeDtypeStruct((ROWS, B), jnp.bfloat16),
            jax.ShapeDtypeStruct((2, ROWS, B), jnp.float32),
            jax.ShapeDtypeStruct((2, ROWS, B), jnp.bfloat16),
        ),
        in_specs=[smem] * 2 + [VMEM] * 7,
        out_specs=(pl.BlockSpec(memory_space=pltpu.HBM),) * 3,
        scratch_shapes=[
            pltpu.VMEM((B, B), jnp.bfloat16),
            pltpu.VMEM((2, B, B), jnp.float32),
            pltpu.VMEM((B, B), jnp.bfloat16),
            pltpu.VMEM((ROWS, B), jnp.bfloat16),
            pltpu.VMEM((ROWS, B), jnp.bfloat16),
            pltpu.VMEM((3, B, B), jnp.float32),
            pltpu.SemaphoreType.DMA((5,)),
        ],
        compiler_params=pltpu.CompilerParams(vmem_limit_bytes=16 << 20),
        cost_estimate=pl.CostEstimate(flops=18 * 2 * B**3, bytes_accessed=6 << 20, transcendentals=0),
    )(decays, refresh, *arrays)


def places():
    return {name: lax.axis_index(name) for name in EVERY}


def cut_kernel(cotangents, activations, *rest):
    outs, other, held, sem = rest[:4], rest[4], rest[5], rest[6]
    at = places()
    spot = (at["y"], at["x_hi"] * 2 + at["x_lo"])
    copies = []

    def copy(src, dst):
        copies.append(pltpu.make_async_copy(src, dst, sem.at[len(copies)]))
        copies[-1].start()

    copy(activations, held)
    pieces = [(at["core"], out) for out in outs] + [(1 - at["core"], other.at[i]) for i in range(4)]
    for (core, out), k in zip(pieces, ORDER * 2):
        for j in range(4):
            start = jnp.where(
                core == 0,
                lax.rem(spot[0] + k, 4) * (4 * B) + j * HALF,
                lax.rem(spot[1] + k, 4) * HALF + (4 * j + 2) * B,
            )
            columns = pl.ds(pl.multiple_of(start, HALF), HALF)
            copy(cotangents.at[:, columns], out.at[:, j * HALF : (j + 1) * HALF])
    copies[0].wait()
    for core, out in pieces:
        out[:, 2 * B :] = held[...]
    for c in copies[1:]:
        c.wait()


def cut(cotangents, activations):
    free = pl.BlockSpec(memory_space=pltpu.HBM)
    cotangents = pltpu.with_memory_space_constraint(cotangents, pltpu.HBM)
    activations = pltpu.with_memory_space_constraint(activations, pltpu.HBM)
    return pl.pallas_call(
        cut_kernel,
        name="cut",
        out_shape=(jax.ShapeDtypeStruct((TOKENS, WIDE), jnp.bfloat16),) * 4
        + (jax.ShapeDtypeStruct((4, TOKENS, WIDE), jnp.bfloat16),),
        in_specs=[free, free],
        out_specs=(VMEM,) * 5,
        scratch_shapes=[pltpu.VMEM((TOKENS, B), jnp.bfloat16), pltpu.SemaphoreType.DMA((33,))],
        compiler_params=pltpu.CompilerParams(vmem_limit_bytes=4 << 20),
        cost_estimate=pl.CostEstimate(flops=0, bytes_accessed=6 << 20, transcendentals=0),
    )(cotangents, activations)


def split_kernel(pieces, *outs):
    for i, out in enumerate(outs):
        out[...] = pieces[i]


def split(pieces):
    return pl.pallas_call(
        split_kernel,
        name="split",
        out_shape=(jax.ShapeDtypeStruct((TOKENS, WIDE), jnp.bfloat16),) * 4,
        in_specs=[VMEM],
        out_specs=(VMEM,) * 4,
        compiler_params=pltpu.CompilerParams(vmem_limit_bytes=1 << 20),
        cost_estimate=pl.CostEstimate(flops=0, bytes_accessed=3 << 20, transcendentals=0),
    )(pieces)


def product_kernel(count, *refs):
    parts, before, outs = refs[:count], refs[count:-4], refs[-4:]
    at = places()
    me = jnp.where(at["core"] == 0, at["x_hi"] * 2 + at["x_lo"], at["y"])
    right = jnp.concatenate([p[:, 2 * B :] for p in parts], axis=0)
    for i, out in enumerate(outs):
        columns = pl.ds(pl.multiple_of(lax.rem(me + ORDER[i], 4) * HALF, HALF), HALF)
        left = jnp.concatenate([p[:, columns] for p in parts], axis=0)
        total = dot(left, right, (0, 0))
        if before:
            total += before[i][...]
        out[...] = total.astype(out.dtype)


def product(parts, before=()):
    send = SEND if before else jnp.float32
    return pl.pallas_call(
        functools.partial(product_kernel, len(parts)),
        name="product",
        out_shape=(jax.ShapeDtypeStruct((HALF, B), send),) * 3 + (jax.ShapeDtypeStruct((HALF, B), jnp.float32),),
        in_specs=[VMEM] * (len(parts) + len(before)),
        out_specs=(VMEM,) * 4,
        compiler_params=pltpu.CompilerParams(vmem_limit_bytes=8 << 20),
        cost_estimate=pl.CostEstimate(flops=len(parts) * B**3, bytes_accessed=4 << 20, transcendentals=0),
    )(*parts, *before)


def plane_sum_kernel(first, second, third, own, keep, near, far):
    total = own[...]
    for part in (first, second, third):
        total += part[...].astype(jnp.float32)
    core = lax.axis_index("core")
    stays = core == lax.axis_index("z_hi")

    @pl.when(core == 0)
    def _():
        keep[...] = total[:ROWS]
        far[...] = total[ROWS:].astype(SEND)

    @pl.when(core == 1)
    def _():
        keep[...] = total[ROWS:]
        far[...] = total[:ROWS].astype(SEND)

    @pl.when(stays)
    def _():
        near[...] = far[...]

    @pl.when(jnp.logical_not(stays))
    def _():
        near[...] = keep[...].astype(SEND)


def plane_sum(parts):
    return pl.pallas_call(
        plane_sum_kernel,
        name="plane_sum",
        out_shape=(
            jax.ShapeDtypeStruct((ROWS, B), jnp.float32),
            jax.ShapeDtypeStruct((ROWS, B), SEND),
            jax.ShapeDtypeStruct((ROWS, B), SEND),
        ),
        in_specs=[VMEM] * 4,
        out_specs=(VMEM,) * 3,
        compiler_params=pltpu.CompilerParams(vmem_limit_bytes=2 << 20),
        cost_estimate=pl.CostEstimate(flops=8 * ROWS * B, bytes_accessed=2 << 20, transcendentals=0),
    )(*parts)


def mirror_sum_kernel(keep, near, far, out):
    stays = lax.axis_index("core") == lax.axis_index("z_hi")

    @pl.when(stays)
    def _():
        out[...] = narrow(keep[...] + near[...].astype(jnp.float32))

    @pl.when(jnp.logical_not(stays))
    def _():
        out[...] = narrow(far[...].astype(jnp.float32) + near[...].astype(jnp.float32))


def mirror_sum(keep, near, far):
    return pl.pallas_call(
        mirror_sum_kernel,
        name="mirror_sum",
        out_shape=jax.ShapeDtypeStruct((ROWS, B), jnp.bfloat16),
        in_specs=[VMEM] * 3,
        out_specs=VMEM,
        compiler_params=pltpu.CompilerParams(vmem_limit_bytes=1 << 20),
        cost_estimate=pl.CostEstimate(flops=2 * ROWS * B, bytes_accessed=1 << 19, transcendentals=0),
    )(keep, near, far)


def quarter_rows(at, a, b):
    top = ((at["x_lo"] ^ a) * 2 + (at["core"] ^ b)) * ROWS
    return pl.ds(pl.multiple_of(top, ROWS), ROWS)


def assemble_kernel(own, p0, p1, p2, p3, full, right):
    at = places()
    for a in range(2):
        for b in range(2):
            pack = (p0, p1, p2, p3)[2 * b + a]
            here = quarter_rows(at, a, b)
            right[here, :] = pack[2]
            for layer in range(2):
                full[layer, here, :] = pack[layer].astype(jnp.float32) if a + b else own[layer]


def assemble(own, packs):
    return pl.pallas_call(
        assemble_kernel,
        name="assemble",
        out_shape=(jax.ShapeDtypeStruct((2, B, B), jnp.float32), jax.ShapeDtypeStruct((B, B), jnp.bfloat16)),
        in_specs=[VMEM] * 5,
        out_specs=(VMEM,) * 2,
        compiler_params=pltpu.CompilerParams(vmem_limit_bytes=1 << 20),
        cost_estimate=pl.CostEstimate(flops=0, bytes_accessed=4 << 20, transcendentals=0),
    )(own, *packs)


def per_device(activations, cotangents, statistics, roots, ages, refresh):
    decays = decay_base ** ages.astype(jnp.float32)
    *own_pieces, other = cut(cotangents, activations)
    own_came = [shift(own_pieces[i], True, ORDER[i]) for i in range(3)]
    pieces = split(partner(other, "core"))
    came = [shift(pieces[i], True, ORDER[i]) for i in range(3)]

    early = product([own_pieces[3], pieces[3]] + own_came)
    *sends, own = product(came, early)
    came = [shift(sends[i], False, ORDER[i]) for i in range(3)]
    pack = jnp.concatenate([narrow(statistics), roots[1:]], axis=0)
    own, pack_core = lax.optimization_barrier((own, partner(pack, "core")))
    keep, near, far = plane_sum(came + [own])
    keep, near, far, pack = lax.optimization_barrier((keep, near, far, pack))
    part = mirror_sum(keep, *mirror(near, far))
    pack_x = partner(pack, "x_lo")
    part = rounded(part.astype(jnp.float32) + swap_z(part, 1).astype(jnp.float32))
    part, pack_x = lax.optimization_barrier((part, pack_x))
    part = rounded(part.astype(jnp.float32) + swap_z(part, 2).astype(jnp.float32))
    part_x, part_core = partner(part, "x_lo"), partner(part, "core")
    grads = (part, part_x, part_core, partner(part_x, "core"))
    full, right = assemble(statistics, (pack, pack_x, pack_core, partner(pack_x, "core")))
    return finish(decays, refresh, *grads, full, right, roots[0])


def solution(mesh):
    split = Mesh(mesh.devices.reshape(4, 4, 2, 2, 2, 2), EVERY)
    placed = (P(EVERY, None), P(EVERY, None), P(None, SHARD, None), P(None, SHARD, None), P(), P())
    return jax.shard_map(
        per_device,
        mesh=split,
        in_specs=placed,
        out_specs=(P(SHARD, None), P(None, SHARD, None), P(None, SHARD, None)),
        check_vma=False,
    )
```

```python
import functools
import math

import jax
import jax.numpy as jnp
from jax import lax
from jax.experimental import pallas as pl
from jax.experimental.pallas import tpu as pltpu
from jax.sharding import Mesh
from jax.sharding import PartitionSpec as P

X = ("x_hi", "x_lo")
Z = ("z_lo", "z_hi")
SHARD = ("y", "z_hi", "x_hi", "x_lo", "core")
EVERY = ("z_lo",) + SHARD

B = 512
ROWS = 128
TOKENS = 128
PART = 64
HALF = B // 2
ORDER = (2, 1, 3, 0)
WIDE = 3 * B
SEND = jnp.bfloat16
VMEM = pl.BlockSpec(memory_space=pltpu.VMEM)

decay_base = 0.9
tiny_term = 1e-06


def shift(x, along_y, by):
    pairs = []
    for y in range(4):
        for x_at in range(4):
            for core in range(2):
                moves_y = (core == 0) == along_y
                to = ((y + by) % 4, x_at) if moves_y else (y, (x_at + by) % 4)
                pairs.append(((y * 4 + x_at) * 2 + core, (to[0] * 4 + to[1]) * 2 + core))
    return lax.ppermute(x, ("y",) + X + ("core",), pairs)


def ring_spot(z, core=None):
    spot = (z % 4) * 2 + z // 4
    return spot if core is None else spot * 2 + core


def swap_z(x, bits):
    return lax.ppermute(x, Z, [(ring_spot(z), ring_spot(z ^ bits)) for z in range(8)])


def mirror(near, far):
    first, second = [], []
    for z in range(8):
        stays = z // 4
        across = (6 + 2 * (z % 2) - z) % 8
        first.append((ring_spot(z, stays), ring_spot(z, 1 - stays)))
        first.append((ring_spot(z, 1 - stays), ring_spot(across, 1 - stays)))
        second.append((ring_spot(z, 1 - stays), ring_spot(across, stays)))
    axes = Z + ("core",)
    return lax.ppermute(near, axes, first), lax.ppermute(far, axes, second)


def diagonal(x):
    pairs = [(z * 2 + a, (z ^ 1) * 2 + 1 - a) for z in range(4) for a in range(2)]
    return lax.ppermute(x, ("z_lo", "x_lo"), pairs)


def partner(x, axis, bits=1):
    n = lax.axis_size(axis)
    return lax.ppermute(x, axis, [(i, i ^ bits) for i in range(n)])


def dot(a, b, contract=(1, 0)):
    dims = (((contract[0],), (contract[1],)), ((), ()))
    return lax.dot_general(a, b, dims, preferred_element_type=jnp.float32)


def narrow(x):
    return x.astype(jnp.bfloat16)


def rounded(x):
    return lax.optimization_barrier(narrow(x))


def finish_kernel(decays, refresh, g_own, g_core, old_stats, old_right, left_old,
                  update, new_stats, new_roots, grad, full, right, left, result, work, sem):
    at = places()
    quarter = at["x_lo"] * 2 + at["core"]
    own = quarter_rows(at, 0, 0)
    factor = 2 * (at["y"] * 4 + at["z_hi"] * 2 + at["x_hi"])
    decay = (decays[factor], decays[factor + 1])
    fresh = (refresh[factor], refresh[factor + 1])
    side = lax.rem(at["z_lo"], 2)
    for i in range(4):
        for b, pieces in enumerate((g_own, g_core)):
            top = ((at["x_lo"] ^ (i // 2)) * 2 + (at["core"] ^ b)) * ROWS + (side ^ (i % 2)) * PART
            grad[pl.ds(pl.multiple_of(top, PART), PART), :] = pieces[i]
    g = grad[...]
    writes = []

    def write(i, src, dst):
        writes.append(pltpu.make_async_copy(src, dst, sem.at[i]))
        writes[-1].start()

    def refresh_stats(layer, gram):
        old = old_stats[layer]
        d = decay[layer]
        a = jnp.where(fresh[layer] == 1, d * old + (1.0 - d) * gram, old)
        full[layer] = a
        write(layer, full.at[layer, own, :], new_stats.at[layer])
        total = jnp.sum(jnp.sum(a * a, axis=0, keepdims=True), axis=1, keepdims=True)
        scaling = 2.5 / jnp.sqrt(total + tiny_term)
        return scaling * a, jnp.sqrt(jnp.sqrt(scaling))

    def both(f, *pairs):
        return f(*(p[0] for p in pairs)), f(*(p[1] for p in pairs))

    def advance(m):
        mb = both(narrow, m)
        square = both(dot, mb, mb)
        u = both(lambda s, v: narrow(s * 0.0625 - 0.625 * v), square, m)
        w = both(dot, u, mb)
        wb = both(narrow, w)
        last = both(dot, u, wb)
        return both(lambda v, w, t: 2.44140625 * v + 3.125 * w + t, m, w, last), mb

    def spread(shape, row0):
        r = lax.broadcasted_iota(jnp.int32, shape, 0) + row0
        c = lax.broadcasted_iota(jnp.int32, shape, 1)
        return jnp.where(r == c, 1.953125, 0.0)

    grams = (dot(g, g, (1, 1)), dot(g, g, (0, 0)))
    m, scale = zip(refresh_stats(0, grams[0]), refresh_stats(1, grams[1]))
    work[0] = m[0]
    m2, mb = advance(m)
    work[1] = m2[0]
    m3, m2b = advance(m2)
    work[2] = m3[0]
    m3b = both(narrow, m3)
    rows = [work[i, own, :] for i in range(3)]
    first = (rows[0], m[1]), (rows[1], m2[1]), (rows[2], m3[1])
    product = dot(narrow(rows[0]), m2b[0]), dot(mb[1], m2b[1])
    y = both(lambda p, v, v2: p * 0.0625 - 0.3125 * (v + v2), product, first[0], first[1])
    product = both(dot, both(narrow, y), m3b)
    diagonal = spread((ROWS, B), quarter * ROWS), spread((B, B), 0)
    out = both(
        lambda e, v, v3, p, s: narrow(s * (e + 1.25 * v - 0.390625 * v3 - 0.25 * p)),
        diagonal, y, first[2], product, scale,
    )
    left[...] = jnp.where(fresh[0] == 1, out[0], left_old[...])
    write(2, left, new_roots.at[0])
    right[...] = jnp.where(fresh[1] == 1, out[1], old_right[...])
    write(3, right.at[own, :], new_roots.at[1])
    mixed = narrow(dot(g, right[...]))
    result[...] = narrow(dot(left[...], mixed) * math.sqrt(B))
    write(4, result, update)
    for w in writes:
        w.wait()


def finish(decays, refresh, *arrays):
    smem = pl.BlockSpec(memory_space=pltpu.SMEM)
    return pl.pallas_call(
        finish_kernel,
        name="finish",
        out_shape=(
            jax.ShapeDtypeStruct((ROWS, B), jnp.bfloat16),
            jax.ShapeDtypeStruct((2, ROWS, B), jnp.float32),
            jax.ShapeDtypeStruct((2, ROWS, B), jnp.bfloat16),
        ),
        in_specs=[smem] * 2 + [VMEM] * 5,
        out_specs=(pl.BlockSpec(memory_space=pltpu.HBM),) * 3,
        scratch_shapes=[
            pltpu.VMEM((B, B), jnp.bfloat16),
            pltpu.VMEM((2, B, B), jnp.float32),
            pltpu.VMEM((B, B), jnp.bfloat16),
            pltpu.VMEM((ROWS, B), jnp.bfloat16),
            pltpu.VMEM((ROWS, B), jnp.bfloat16),
            pltpu.VMEM((3, B, B), jnp.float32),
            pltpu.SemaphoreType.DMA((5,)),
        ],
        compiler_params=pltpu.CompilerParams(vmem_limit_bytes=16 << 20),
        cost_estimate=pl.CostEstimate(flops=18 * 2 * B**3, bytes_accessed=6 << 20, transcendentals=0),
    )(decays, refresh, *arrays)


def places():
    return {name: lax.axis_index(name) for name in EVERY}


def cut_kernel(cotangents, activations, *rest):
    outs, other, held, sem = rest[:4], rest[4], rest[5], rest[6]
    at = places()
    spot = (at["y"], at["x_hi"] * 2 + at["x_lo"])
    copies = []

    def copy(src, dst):
        copies.append(pltpu.make_async_copy(src, dst, sem.at[len(copies)]))
        copies[-1].start()

    copy(activations, held)
    pieces = [(at["core"], out) for out in outs] + [(1 - at["core"], other.at[i]) for i in range(4)]
    for (core, out), k in zip(pieces, ORDER * 2):
        for j in range(4):
            start = jnp.where(
                core == 0,
                lax.rem(spot[0] + k, 4) * (4 * B) + j * HALF,
                lax.rem(spot[1] + k, 4) * HALF + (4 * j + 2) * B,
            )
            columns = pl.ds(pl.multiple_of(start, HALF), HALF)
            copy(cotangents.at[:, columns], out.at[:, j * HALF : (j + 1) * HALF])
    copies[0].wait()
    for core, out in pieces:
        out[:, 2 * B :] = held[...]
    for c in copies[1:]:
        c.wait()


def cut(cotangents, activations):
    free = pl.BlockSpec(memory_space=pltpu.HBM)
    cotangents = pltpu.with_memory_space_constraint(cotangents, pltpu.HBM)
    activations = pltpu.with_memory_space_constraint(activations, pltpu.HBM)
    return pl.pallas_call(
        cut_kernel,
        name="cut",
        out_shape=(jax.ShapeDtypeStruct((TOKENS, WIDE), jnp.bfloat16),) * 4
        + (jax.ShapeDtypeStruct((4, TOKENS, WIDE), jnp.bfloat16),),
        in_specs=[free, free],
        out_specs=(VMEM,) * 5,
        scratch_shapes=[pltpu.VMEM((TOKENS, B), jnp.bfloat16), pltpu.SemaphoreType.DMA((33,))],
        compiler_params=pltpu.CompilerParams(vmem_limit_bytes=4 << 20),
        cost_estimate=pl.CostEstimate(flops=0, bytes_accessed=6 << 20, transcendentals=0),
    )(cotangents, activations)


def split_kernel(pieces, *outs):
    for i, out in enumerate(outs):
        out[...] = pieces[i]


def split(pieces):
    return pl.pallas_call(
        split_kernel,
        name="split",
        out_shape=(jax.ShapeDtypeStruct((TOKENS, WIDE), jnp.bfloat16),) * 4,
        in_specs=[VMEM],
        out_specs=(VMEM,) * 4,
        compiler_params=pltpu.CompilerParams(vmem_limit_bytes=1 << 20),
        cost_estimate=pl.CostEstimate(flops=0, bytes_accessed=3 << 20, transcendentals=0),
    )(pieces)


def product_kernel(count, *refs):
    parts, before, outs = refs[:count], refs[count:-4], refs[-4:]
    at = places()
    me = jnp.where(at["core"] == 0, at["x_hi"] * 2 + at["x_lo"], at["y"])
    right = jnp.concatenate([p[:, 2 * B :] for p in parts], axis=0)
    for i, out in enumerate(outs):
        columns = pl.ds(pl.multiple_of(lax.rem(me + ORDER[i], 4) * HALF, HALF), HALF)
        left = jnp.concatenate([p[:, columns] for p in parts], axis=0)
        total = dot(left, right, (0, 0))
        if before:
            total += before[i][...]
        out[...] = total.astype(out.dtype)


def product(parts, before=()):
    send = SEND if before else jnp.float32
    return pl.pallas_call(
        functools.partial(product_kernel, len(parts)),
        name="product",
        out_shape=(jax.ShapeDtypeStruct((HALF, B), send),) * 3 + (jax.ShapeDtypeStruct((HALF, B), jnp.float32),),
        in_specs=[VMEM] * (len(parts) + len(before)),
        out_specs=(VMEM,) * 4,
        compiler_params=pltpu.CompilerParams(vmem_limit_bytes=8 << 20),
        cost_estimate=pl.CostEstimate(flops=len(parts) * B**3, bytes_accessed=4 << 20, transcendentals=0),
    )(*parts, *before)


def plane_sum_kernel(first, second, third, own, keep, send, total):
    t = own[...]
    for part in (first, second, third):
        t += part[...].astype(jnp.float32)
    total[...] = t
    side = lax.rem(lax.axis_index("z_lo"), 2)
    for i in range(2):
        here = pl.ds(pl.multiple_of(i * ROWS + side * PART, PART), PART)
        there = pl.ds(pl.multiple_of(i * ROWS + (1 - side) * PART, PART), PART)
        keep[i] = total[here, :]
        send[i] = total[there, :].astype(SEND)


def plane_sum(parts):
    return pl.pallas_call(
        plane_sum_kernel,
        name="plane_sum",
        out_shape=(
            jax.ShapeDtypeStruct((2, PART, B), jnp.float32),
            jax.ShapeDtypeStruct((2, PART, B), SEND),
        ),
        in_specs=[VMEM] * 4,
        out_specs=(VMEM,) * 2,
        scratch_shapes=[pltpu.VMEM((HALF, B), jnp.float32)],
        compiler_params=pltpu.CompilerParams(vmem_limit_bytes=2 << 20),
        cost_estimate=pl.CostEstimate(flops=8 * ROWS * B, bytes_accessed=2 << 20, transcendentals=0),
    )(*parts)


def pair_sum_kernel(keep, came, base, near, far):
    core = lax.axis_index("core")
    mine = keep[core] + came[core].astype(jnp.float32)
    other = (keep[1 - core] + came[1 - core].astype(jnp.float32)).astype(SEND)
    base[...] = mine
    far[...] = other
    stays = core == lax.axis_index("z_hi")

    @pl.when(stays)
    def _():
        near[...] = other

    @pl.when(jnp.logical_not(stays))
    def _():
        near[...] = mine.astype(SEND)


def pair_sum(keep, came):
    return pl.pallas_call(
        pair_sum_kernel,
        name="pair_sum",
        out_shape=(
            jax.ShapeDtypeStruct((PART, B), jnp.float32),
            jax.ShapeDtypeStruct((PART, B), SEND),
            jax.ShapeDtypeStruct((PART, B), SEND),
        ),
        in_specs=[VMEM] * 2,
        out_specs=(VMEM,) * 3,
        compiler_params=pltpu.CompilerParams(vmem_limit_bytes=1 << 20),
        cost_estimate=pl.CostEstimate(flops=2 * ROWS * B, bytes_accessed=1 << 20, transcendentals=0),
    )(keep, came)


def mirror_sum_kernel(base, near, far, out):
    stays = lax.axis_index("core") == lax.axis_index("z_hi")

    @pl.when(stays)
    def _():
        out[...] = narrow(base[...] + near[...].astype(jnp.float32))

    @pl.when(jnp.logical_not(stays))
    def _():
        out[...] = narrow(far[...].astype(jnp.float32) + near[...].astype(jnp.float32))


def mirror_sum(base, near, far):
    return pl.pallas_call(
        mirror_sum_kernel,
        name="mirror_sum",
        out_shape=jax.ShapeDtypeStruct((PART, B), jnp.bfloat16),
        in_specs=[VMEM] * 3,
        out_specs=VMEM,
        compiler_params=pltpu.CompilerParams(vmem_limit_bytes=1 << 20),
        cost_estimate=pl.CostEstimate(flops=2 * PART * B, bytes_accessed=1 << 19, transcendentals=0),
    )(base, near, far)


def stack_kernel(*refs):
    for i, ref in enumerate(refs[:-1]):
        refs[-1][i] = ref[...]


def stack(parts):
    return pl.pallas_call(
        stack_kernel,
        name="stack",
        out_shape=jax.ShapeDtypeStruct((len(parts),) + parts[0].shape, parts[0].dtype),
        in_specs=[VMEM] * len(parts),
        out_specs=VMEM,
        compiler_params=pltpu.CompilerParams(vmem_limit_bytes=1 << 20),
        cost_estimate=pl.CostEstimate(flops=0, bytes_accessed=1 << 19, transcendentals=0),
    )(*parts)


def quarter_rows(at, a, b):
    top = ((at["x_lo"] ^ a) * 2 + (at["core"] ^ b)) * ROWS
    return pl.ds(pl.multiple_of(top, ROWS), ROWS)


def assemble_kernel(own, p0, p1, p2, p3, full, right):
    at = places()
    for a in range(2):
        for b in range(2):
            pack = (p0, p1, p2, p3)[2 * b + a]
            here = quarter_rows(at, a, b)
            right[here, :] = pack[2]
            for layer in range(2):
                full[layer, here, :] = pack[layer].astype(jnp.float32) if a + b else own[layer]


def assemble(own, packs):
    return pl.pallas_call(
        assemble_kernel,
        name="assemble",
        out_shape=(jax.ShapeDtypeStruct((2, B, B), jnp.float32), jax.ShapeDtypeStruct((B, B), jnp.bfloat16)),
        in_specs=[VMEM] * 5,
        out_specs=(VMEM,) * 2,
        compiler_params=pltpu.CompilerParams(vmem_limit_bytes=1 << 20),
        cost_estimate=pl.CostEstimate(flops=0, bytes_accessed=4 << 20, transcendentals=0),
    )(own, *packs)


def per_device(activations, cotangents, statistics, roots, ages, refresh):
    decays = decay_base ** ages.astype(jnp.float32)
    *own_pieces, other = cut(cotangents, activations)
    own_came = [shift(own_pieces[i], True, ORDER[i]) for i in range(3)]
    pieces = split(partner(other, "core"))
    came = [shift(pieces[i], True, ORDER[i]) for i in range(3)]

    early = product([own_pieces[3], pieces[3]] + own_came)
    *sends, own = product(came, early)
    came = [shift(sends[i], False, ORDER[i]) for i in range(3)]
    pack = jnp.concatenate([narrow(statistics), roots[1:]], axis=0)
    own, pack_core = lax.optimization_barrier((own, partner(pack, "core")))
    keep, send = plane_sum(came + [own])
    keep, send, pack = lax.optimization_barrier((keep, send, pack))
    base, near, far = pair_sum(keep, swap_z(send, 1))
    pack_x = partner(pack, "x_lo")
    part, pack_x = lax.optimization_barrier((mirror_sum(base, *mirror(near, far)), pack_x))
    part = rounded(part.astype(jnp.float32) + swap_z(part, 2).astype(jnp.float32))
    grad = stack((part, swap_z(part, 1), partner(part, "x_lo"), diagonal(part)))
    grads = (grad, partner(grad, "core"))
    full, right = assemble(statistics, (pack, pack_x, pack_core, partner(pack_x, "core")))
    return finish(decays, refresh, *grads, full, right, roots[0])


def solution(mesh):
    split = Mesh(mesh.devices.reshape(4, 4, 2, 2, 2, 2), EVERY)
    placed = (P(EVERY, None), P(EVERY, None), P(None, SHARD, None), P(None, SHARD, None), P(), P())
    return jax.shard_map(
        per_device,
        mesh=split,
        in_specs=placed,
        out_specs=(P(SHARD, None), P(None, SHARD, None), P(None, SHARD, None)),
        check_vma=False,
    )
```

```python
import functools
import math

import jax
import jax.numpy as jnp
from jax import lax
from jax.experimental import pallas as pl
from jax.experimental.pallas import tpu as pltpu
from jax.sharding import Mesh
from jax.sharding import PartitionSpec as P

X = ("x_hi", "x_lo")
Z = ("z_lo", "z_hi")
SHARD = ("y", "z_hi", "x_hi", "x_lo", "core")
EVERY = ("z_lo",) + SHARD

B = 512
ROWS = 128
TOKENS = 128
PART = 64
HALF = B // 2
ORDER = (2, 1, 3, 0)
WIDE = 3 * B
SEND = jnp.bfloat16
VMEM = pl.BlockSpec(memory_space=pltpu.VMEM)

decay_base = 0.9
tiny_term = 1e-06


def shift(x, along_y, by):
    pairs = []
    for y in range(4):
        for x_at in range(4):
            for core in range(2):
                moves_y = (core == 0) == along_y
                to = ((y + by) % 4, x_at) if moves_y else (y, (x_at + by) % 4)
                pairs.append(((y * 4 + x_at) * 2 + core, (to[0] * 4 + to[1]) * 2 + core))
    return lax.ppermute(x, ("y",) + X + ("core",), pairs)


def ring_spot(z):
    return (z % 4) * 2 + z // 4


def swap_z(x, bits):
    return lax.ppermute(x, Z, [(ring_spot(z), ring_spot(z ^ bits)) for z in range(8)])


def cross_z(x):
    return lax.ppermute(x, Z, [(ring_spot(z), ring_spot((6 + 2 * (z % 2) - z) % 8)) for z in range(8)])


def diagonal(x):
    pairs = [(z * 2 + a, (z ^ 1) * 2 + 1 - a) for z in range(4) for a in range(2)]
    return lax.ppermute(x, ("z_lo", "x_lo"), pairs)


def partner(x, axis, bits=1):
    n = lax.axis_size(axis)
    return lax.ppermute(x, axis, [(i, i ^ bits) for i in range(n)])


def dot(a, b, contract=(1, 0)):
    dims = (((contract[0],), (contract[1],)), ((), ()))
    return lax.dot_general(a, b, dims, preferred_element_type=jnp.float32)


def narrow(x):
    return x.astype(jnp.bfloat16)


def rounded(x):
    return lax.optimization_barrier(narrow(x))


def finish_kernel(decays, refresh, g_own, g_core, old_stats, old_right, left_old,
                  update, new_stats, new_roots, grad, full, right, left, result, work, sem):
    at = places()
    quarter = at["x_lo"] * 2 + at["core"]
    own = quarter_rows(at, 0, 0)
    factor = 2 * (at["y"] * 4 + at["z_hi"] * 2 + at["x_hi"])
    decay = (decays[factor], decays[factor + 1])
    fresh = (refresh[factor], refresh[factor + 1])
    side = lax.rem(at["z_lo"], 2)
    for i in range(4):
        for b, pieces in enumerate((g_own, g_core)):
            top = ((at["x_lo"] ^ (i // 2)) * 2 + (at["core"] ^ b)) * ROWS + (side ^ (i % 2)) * PART
            grad[pl.ds(pl.multiple_of(top, PART), PART), :] = pieces[i]
    g = grad[...]
    writes = []

    def write(i, src, dst):
        writes.append(pltpu.make_async_copy(src, dst, sem.at[i]))
        writes[-1].start()

    def refresh_stats(layer, gram):
        old = old_stats[layer]
        d = decay[layer]
        a = jnp.where(fresh[layer] == 1, d * old + (1.0 - d) * gram, old)
        full[layer] = a
        write(layer, full.at[layer, own, :], new_stats.at[layer])
        total = jnp.sum(jnp.sum(a * a, axis=0, keepdims=True), axis=1, keepdims=True)
        scaling = 2.5 / jnp.sqrt(total + tiny_term)
        return scaling * a, jnp.sqrt(jnp.sqrt(scaling))

    def both(f, *pairs):
        return f(*(p[0] for p in pairs)), f(*(p[1] for p in pairs))

    def advance(m):
        mb = both(narrow, m)
        square = both(dot, mb, mb)
        u = both(lambda s, v: narrow(s * 0.0625 - 0.625 * v), square, m)
        w = both(dot, u, mb)
        wb = both(narrow, w)
        last = both(dot, u, wb)
        return both(lambda v, w, t: 2.44140625 * v + 3.125 * w + t, m, w, last), mb

    def spread(shape, row0):
        r = lax.broadcasted_iota(jnp.int32, shape, 0) + row0
        c = lax.broadcasted_iota(jnp.int32, shape, 1)
        return jnp.where(r == c, 1.953125, 0.0)

    grams = (dot(g, g, (1, 1)), dot(g, g, (0, 0)))
    m, scale = zip(refresh_stats(0, grams[0]), refresh_stats(1, grams[1]))
    work[0] = m[0]
    m2, mb = advance(m)
    work[1] = m2[0]
    m3, m2b = advance(m2)
    work[2] = m3[0]
    m3b = both(narrow, m3)
    rows = [work[i, own, :] for i in range(3)]
    first = (rows[0], m[1]), (rows[1], m2[1]), (rows[2], m3[1])
    product = dot(narrow(rows[0]), m2b[0]), dot(mb[1], m2b[1])
    y = both(lambda p, v, v2: p * 0.0625 - 0.3125 * (v + v2), product, first[0], first[1])
    product = both(dot, both(narrow, y), m3b)
    diagonal = spread((ROWS, B), quarter * ROWS), spread((B, B), 0)
    out = both(
        lambda e, v, v3, p, s: narrow(s * (e + 1.25 * v - 0.390625 * v3 - 0.25 * p)),
        diagonal, y, first[2], product, scale,
    )
    left[...] = jnp.where(fresh[0] == 1, out[0], left_old[...])
    write(2, left, new_roots.at[0])
    right[...] = jnp.where(fresh[1] == 1, out[1], old_right[...])
    write(3, right.at[own, :], new_roots.at[1])
    mixed = narrow(dot(g, right[...]))
    result[...] = narrow(dot(left[...], mixed) * math.sqrt(B))
    write(4, result, update)
    for w in writes:
        w.wait()


def finish(decays, refresh, *arrays):
    smem = pl.BlockSpec(memory_space=pltpu.SMEM)
    return pl.pallas_call(
        finish_kernel,
        name="finish",
        out_shape=(
            jax.ShapeDtypeStruct((ROWS, B), jnp.bfloat16),
            jax.ShapeDtypeStruct((2, ROWS, B), jnp.float32),
            jax.ShapeDtypeStruct((2, ROWS, B), jnp.bfloat16),
        ),
        in_specs=[smem] * 2 + [VMEM] * 5,
        out_specs=(pl.BlockSpec(memory_space=pltpu.HBM),) * 3,
        scratch_shapes=[
            pltpu.VMEM((B, B), jnp.bfloat16),
            pltpu.VMEM((2, B, B), jnp.float32),
            pltpu.VMEM((B, B), jnp.bfloat16),
            pltpu.VMEM((ROWS, B), jnp.bfloat16),
            pltpu.VMEM((ROWS, B), jnp.bfloat16),
            pltpu.VMEM((3, B, B), jnp.float32),
            pltpu.SemaphoreType.DMA((5,)),
        ],
        compiler_params=pltpu.CompilerParams(vmem_limit_bytes=16 << 20),
        cost_estimate=pl.CostEstimate(flops=18 * 2 * B**3, bytes_accessed=6 << 20, transcendentals=0),
    )(decays, refresh, *arrays)


def places():
    return {name: lax.axis_index(name) for name in EVERY}


def cut_kernel(cotangents, activations, *rest):
    outs, other, held, sem = rest[:4], rest[4], rest[5], rest[6]
    at = places()
    spot = (at["y"], at["x_hi"] * 2 + at["x_lo"])
    copies = []

    def copy(src, dst):
        copies.append(pltpu.make_async_copy(src, dst, sem.at[len(copies)]))
        copies[-1].start()

    copy(activations, held)
    pieces = [(at["core"], out) for out in outs] + [(1 - at["core"], other.at[i]) for i in range(4)]
    for (core, out), k in zip(pieces, ORDER * 2):
        for j in range(4):
            start = jnp.where(
                core == 0,
                lax.rem(spot[0] + k, 4) * (4 * B) + j * HALF,
                lax.rem(spot[1] + k, 4) * HALF + (4 * j + 2) * B,
            )
            columns = pl.ds(pl.multiple_of(start, HALF), HALF)
            copy(cotangents.at[:, columns], out.at[:, j * HALF : (j + 1) * HALF])
    copies[0].wait()
    for core, out in pieces:
        out[:, 2 * B :] = held[...]
    for c in copies[1:]:
        c.wait()


def cut(cotangents, activations):
    free = pl.BlockSpec(memory_space=pltpu.HBM)
    cotangents = pltpu.with_memory_space_constraint(cotangents, pltpu.HBM)
    activations = pltpu.with_memory_space_constraint(activations, pltpu.HBM)
    return pl.pallas_call(
        cut_kernel,
        name="cut",
        out_shape=(jax.ShapeDtypeStruct((TOKENS, WIDE), jnp.bfloat16),) * 4
        + (jax.ShapeDtypeStruct((4, TOKENS, WIDE), jnp.bfloat16),),
        in_specs=[free, free],
        out_specs=(VMEM,) * 5,
        scratch_shapes=[pltpu.VMEM((TOKENS, B), jnp.bfloat16), pltpu.SemaphoreType.DMA((33,))],
        compiler_params=pltpu.CompilerParams(vmem_limit_bytes=4 << 20),
        cost_estimate=pl.CostEstimate(flops=0, bytes_accessed=6 << 20, transcendentals=0),
    )(cotangents, activations)


def split_kernel(pieces, *outs):
    for i, out in enumerate(outs):
        out[...] = pieces[i]


def split(pieces):
    return pl.pallas_call(
        split_kernel,
        name="split",
        out_shape=(jax.ShapeDtypeStruct((TOKENS, WIDE), jnp.bfloat16),) * 4,
        in_specs=[VMEM],
        out_specs=(VMEM,) * 4,
        compiler_params=pltpu.CompilerParams(vmem_limit_bytes=1 << 20),
        cost_estimate=pl.CostEstimate(flops=0, bytes_accessed=3 << 20, transcendentals=0),
    )(pieces)


def product_kernel(count, *refs):
    parts, before, outs = refs[:count], refs[count:-4], refs[-4:]
    at = places()
    me = jnp.where(at["core"] == 0, at["x_hi"] * 2 + at["x_lo"], at["y"])
    right = jnp.concatenate([p[:, 2 * B :] for p in parts], axis=0)
    for i, out in enumerate(outs):
        columns = pl.ds(pl.multiple_of(lax.rem(me + ORDER[i], 4) * HALF, HALF), HALF)
        left = jnp.concatenate([p[:, columns] for p in parts], axis=0)
        total = dot(left, right, (0, 0))
        if before:
            total += before[i][...]
        out[...] = total.astype(out.dtype)


def product(parts, before=()):
    send = SEND if before else jnp.float32
    return pl.pallas_call(
        functools.partial(product_kernel, len(parts)),
        name="product",
        out_shape=(jax.ShapeDtypeStruct((HALF, B), send),) * 3 + (jax.ShapeDtypeStruct((HALF, B), jnp.float32),),
        in_specs=[VMEM] * (len(parts) + len(before)),
        out_specs=(VMEM,) * 4,
        compiler_params=pltpu.CompilerParams(vmem_limit_bytes=8 << 20),
        cost_estimate=pl.CostEstimate(flops=len(parts) * B**3, bytes_accessed=4 << 20, transcendentals=0),
    )(*parts, *before)


def plane_sum_kernel(first, second, third, own, keep, send, total):
    t = own[...]
    for part in (first, second, third):
        t += part[...].astype(jnp.float32)
    total[...] = t
    side = lax.rem(lax.axis_index("z_lo"), 2)
    for i in range(2):
        here = pl.ds(pl.multiple_of(i * ROWS + side * PART, PART), PART)
        there = pl.ds(pl.multiple_of(i * ROWS + (1 - side) * PART, PART), PART)
        keep[i] = total[here, :]
        send[i] = total[there, :].astype(SEND)


def plane_sum(parts):
    return pl.pallas_call(
        plane_sum_kernel,
        name="plane_sum",
        out_shape=(
            jax.ShapeDtypeStruct((2, PART, B), jnp.float32),
            jax.ShapeDtypeStruct((2, PART, B), SEND),
        ),
        in_specs=[VMEM] * 4,
        out_specs=(VMEM,) * 2,
        scratch_shapes=[pltpu.VMEM((HALF, B), jnp.float32)],
        compiler_params=pltpu.CompilerParams(vmem_limit_bytes=2 << 20),
        cost_estimate=pl.CostEstimate(flops=8 * ROWS * B, bytes_accessed=2 << 20, transcendentals=0),
    )(*parts)


def pair_sum_kernel(keep, came, mine, other):
    core = lax.axis_index("core")
    mine[...] = keep[core] + came[core].astype(jnp.float32)
    other[...] = (keep[1 - core] + came[1 - core].astype(jnp.float32)).astype(SEND)


def pair_sum(keep, came):
    return pl.pallas_call(
        pair_sum_kernel,
        name="pair_sum",
        out_shape=(jax.ShapeDtypeStruct((PART, B), jnp.float32), jax.ShapeDtypeStruct((PART, B), SEND)),
        in_specs=[VMEM] * 2,
        out_specs=(VMEM,) * 2,
        compiler_params=pltpu.CompilerParams(vmem_limit_bytes=1 << 20),
        cost_estimate=pl.CostEstimate(flops=2 * ROWS * B, bytes_accessed=1 << 20, transcendentals=0),
    )(keep, came)


def choose_kernel(mine, came, stay, leave):
    stays = lax.axis_index("core") == lax.axis_index("z_hi")

    @pl.when(stays)
    def _():
        stay[...] = mine[...]
        leave[...] = came[...]

    @pl.when(jnp.logical_not(stays))
    def _():
        stay[...] = came[...].astype(jnp.float32)
        leave[...] = mine[...].astype(SEND)


def choose(mine, came):
    return pl.pallas_call(
        choose_kernel,
        name="choose",
        out_shape=(jax.ShapeDtypeStruct((PART, B), jnp.float32), jax.ShapeDtypeStruct((PART, B), SEND)),
        in_specs=[VMEM] * 2,
        out_specs=(VMEM,) * 2,
        compiler_params=pltpu.CompilerParams(vmem_limit_bytes=1 << 20),
        cost_estimate=pl.CostEstimate(flops=0, bytes_accessed=1 << 19, transcendentals=0),
    )(mine, came)


def stack_kernel(*refs):
    for i, ref in enumerate(refs[:-1]):
        refs[-1][i] = ref[...]


def stack(parts):
    return pl.pallas_call(
        stack_kernel,
        name="stack",
        out_shape=jax.ShapeDtypeStruct((len(parts),) + parts[0].shape, parts[0].dtype),
        in_specs=[VMEM] * len(parts),
        out_specs=VMEM,
        compiler_params=pltpu.CompilerParams(vmem_limit_bytes=1 << 20),
        cost_estimate=pl.CostEstimate(flops=0, bytes_accessed=1 << 19, transcendentals=0),
    )(*parts)


def quarter_rows(at, a, b):
    top = ((at["x_lo"] ^ a) * 2 + (at["core"] ^ b)) * ROWS
    return pl.ds(pl.multiple_of(top, ROWS), ROWS)


def assemble_kernel(own, p0, p1, p2, p3, full, right):
    at = places()
    for a in range(2):
        for b in range(2):
            pack = (p0, p1, p2, p3)[2 * b + a]
            here = quarter_rows(at, a, b)
            right[here, :] = pack[2]
            for layer in range(2):
                full[layer, here, :] = pack[layer].astype(jnp.float32) if a + b else own[layer]


def assemble(own, packs):
    return pl.pallas_call(
        assemble_kernel,
        name="assemble",
        out_shape=(jax.ShapeDtypeStruct((2, B, B), jnp.float32), jax.ShapeDtypeStruct((B, B), jnp.bfloat16)),
        in_specs=[VMEM] * 5,
        out_specs=(VMEM,) * 2,
        compiler_params=pltpu.CompilerParams(vmem_limit_bytes=1 << 20),
        cost_estimate=pl.CostEstimate(flops=0, bytes_accessed=4 << 20, transcendentals=0),
    )(own, *packs)


def per_device(activations, cotangents, statistics, roots, ages, refresh):
    decays = decay_base ** ages.astype(jnp.float32)
    *own_pieces, other = cut(cotangents, activations)
    own_came = [shift(own_pieces[i], True, ORDER[i]) for i in range(3)]
    pieces = split(partner(other, "core"))
    came = [shift(pieces[i], True, ORDER[i]) for i in range(3)]

    early = product([own_pieces[3], pieces[3]] + own_came)
    *sends, own = product(came, early)
    came = [shift(sends[i], False, ORDER[i]) for i in range(3)]
    pack = jnp.concatenate([narrow(statistics), roots[1:]], axis=0)
    own, pack_core = lax.optimization_barrier((own, partner(pack, "core")))
    keep, send = plane_sum(came + [own])
    mine, other = pair_sum(keep, swap_z(send, 1))
    stay, leave = choose(mine, partner(other, "core"))
    stay, leave, pack = lax.optimization_barrier((stay, leave, pack))
    part = rounded(stay + cross_z(leave).astype(jnp.float32))
    pack_x = partner(pack, "x_lo")
    part = rounded(part.astype(jnp.float32) + swap_z(part, 2).astype(jnp.float32))
    part, pack_x = lax.optimization_barrier((part, pack_x))
    grad = stack((part, swap_z(part, 1), partner(part, "x_lo"), diagonal(part)))
    grads = (grad, partner(grad, "core"))
    full, right = assemble(statistics, (pack, pack_x, pack_core, partner(pack_x, "core")))
    return finish(decays, refresh, *grads, full, right, roots[0])


def solution(mesh):
    split = Mesh(mesh.devices.reshape(4, 4, 2, 2, 2, 2), EVERY)
    placed = (P(EVERY, None), P(EVERY, None), P(None, SHARD, None), P(None, SHARD, None), P(), P())
    return jax.shard_map(
        per_device,
        mesh=split,
        in_specs=placed,
        out_specs=(P(SHARD, None), P(None, SHARD, None), P(None, SHARD, None)),
        check_vma=False,
    )
```

```python
import functools
import math

import jax
import jax.numpy as jnp
from jax import lax
from jax.experimental import pallas as pl
from jax.experimental.pallas import tpu as pltpu
from jax.sharding import Mesh
from jax.sharding import PartitionSpec as P

X = ("x_hi", "x_lo")
Z = ("z_lo", "z_hi")
SHARD = ("y", "z_hi", "x_hi", "x_lo", "core")
EVERY = ("z_lo",) + SHARD

B = 512
ROWS = 128
TOKENS = 128
HALF = B // 2
ORDER = (2, 1, 3, 0)
WIDE = 3 * B
SEND = jnp.bfloat16
VMEM = pl.BlockSpec(memory_space=pltpu.VMEM)

decay_base = 0.9
tiny_term = 1e-06


def shift(x, along_y, by):
    pairs = []
    for y in range(4):
        for x_at in range(4):
            for core in range(2):
                moves_y = (core == 0) == along_y
                to = ((y + by) % 4, x_at) if moves_y else (y, (x_at + by) % 4)
                pairs.append(((y * 4 + x_at) * 2 + core, (to[0] * 4 + to[1]) * 2 + core))
    return lax.ppermute(x, ("y",) + X + ("core",), pairs)


def ring_spot(z, core=None):
    spot = (z % 4) * 2 + z // 4
    return spot if core is None else spot * 2 + core


def swap_z(x, bits):
    return lax.ppermute(x, Z, [(ring_spot(z), ring_spot(z ^ bits)) for z in range(8)])


def mirror(near, far):
    first, second = [], []
    for z in range(8):
        stays = z // 4
        first.append((ring_spot(z, stays), ring_spot(z, 1 - stays)))
        across = (6 + 2 * (z % 2) - z) % 8
        first.append((ring_spot(z, 1 - stays), ring_spot(across, 1 - stays)))
        second.append((ring_spot(z, 1 - stays), ring_spot(across, stays)))
    axes = Z + ("core",)
    return lax.ppermute(near, axes, first), lax.ppermute(far, axes, second)


def partner(x, axis, bits=1):
    n = lax.axis_size(axis)
    return lax.ppermute(x, axis, [(i, i ^ bits) for i in range(n)])


def dot(a, b, contract=(1, 0)):
    dims = (((contract[0],), (contract[1],)), ((), ()))
    return lax.dot_general(a, b, dims, preferred_element_type=jnp.float32)


def narrow(x):
    return x.astype(jnp.bfloat16)


def rounded(x):
    return lax.optimization_barrier(narrow(x))


def finish_kernel(decays, refresh, g0, g1, g2, g3, old_stats, old_right, left_old,
                  update, new_stats, new_roots, grad, full, right, left, result, work, sem):
    at = places()
    quarter = at["x_lo"] * 2 + at["core"]
    own = quarter_rows(at, 0, 0)
    factor = 2 * (at["y"] * 4 + at["z_hi"] * 2 + at["x_hi"])
    decay = (decays[factor], decays[factor + 1])
    fresh = (refresh[factor], refresh[factor + 1])
    for a in range(2):
        for b in range(2):
            grad[quarter_rows(at, a, b), :] = (g0, g1, g2, g3)[2 * b + a][...]
    g = grad[...]
    writes = []

    def write(i, src, dst):
        writes.append(pltpu.make_async_copy(src, dst, sem.at[i]))
        writes[-1].start()

    def refresh_stats(layer, gram):
        old = old_stats[layer]
        d = decay[layer]
        a = jnp.where(fresh[layer] == 1, d * old + (1.0 - d) * gram, old)
        full[layer] = a
        write(layer, full.at[layer, own, :], new_stats.at[layer])
        total = jnp.sum(jnp.sum(a * a, axis=0, keepdims=True), axis=1, keepdims=True)
        scaling = 2.5 / jnp.sqrt(total + tiny_term)
        return scaling * a, jnp.sqrt(jnp.sqrt(scaling))

    def both(f, *pairs):
        return f(*(p[0] for p in pairs)), f(*(p[1] for p in pairs))

    def advance(m):
        mb = both(narrow, m)
        square = both(dot, mb, mb)
        u = both(lambda s, v: narrow(s * 0.0625 - 0.625 * v), square, m)
        w = both(dot, u, mb)
        wb = both(narrow, w)
        last = both(dot, u, wb)
        return both(lambda v, w, t: 2.44140625 * v + 3.125 * w + t, m, w, last), mb

    def spread(shape, row0):
        r = lax.broadcasted_iota(jnp.int32, shape, 0) + row0
        c = lax.broadcasted_iota(jnp.int32, shape, 1)
        return jnp.where(r == c, 1.953125, 0.0)

    grams = (dot(g, g, (1, 1)), dot(g, g, (0, 0)))
    m, scale = zip(refresh_stats(0, grams[0]), refresh_stats(1, grams[1]))
    work[0] = m[0]
    m2, mb = advance(m)
    work[1] = m2[0]
    m3, m2b = advance(m2)
    work[2] = m3[0]
    m3b = both(narrow, m3)
    rows = [work[i, own, :] for i in range(3)]
    first = (rows[0], m[1]), (rows[1], m2[1]), (rows[2], m3[1])
    product = dot(narrow(rows[0]), m2b[0]), dot(mb[1], m2b[1])
    y = both(lambda p, v, v2: p * 0.0625 - 0.3125 * (v + v2), product, first[0], first[1])
    product = both(dot, both(narrow, y), m3b)
    diagonal = spread((ROWS, B), quarter * ROWS), spread((B, B), 0)
    out = both(
        lambda e, v, v3, p, s: narrow(s * (e + 1.25 * v - 0.390625 * v3 - 0.25 * p)),
        diagonal, y, first[2], product, scale,
    )
    left[...] = jnp.where(fresh[0] == 1, out[0], left_old[...])
    write(2, left, new_roots.at[0])
    right[...] = jnp.where(fresh[1] == 1, out[1], old_right[...])
    write(3, right.at[own, :], new_roots.at[1])
    mixed = narrow(dot(g, right[...]))
    result[...] = narrow(dot(left[...], mixed) * math.sqrt(B))
    write(4, result, update)
    for w in writes:
        w.wait()


def finish(decays, refresh, *arrays):
    smem = pl.BlockSpec(memory_space=pltpu.SMEM)
    return pl.pallas_call(
        finish_kernel,
        name="finish",
        out_shape=(
            jax.ShapeDtypeStruct((ROWS, B), jnp.bfloat16),
            jax.ShapeDtypeStruct((2, ROWS, B), jnp.float32),
            jax.ShapeDtypeStruct((2, ROWS, B), jnp.bfloat16),
        ),
        in_specs=[smem] * 2 + [VMEM] * 7,
        out_specs=(pl.BlockSpec(memory_space=pltpu.HBM),) * 3,
        scratch_shapes=[
            pltpu.VMEM((B, B), jnp.bfloat16),
            pltpu.VMEM((2, B, B), jnp.float32),
            pltpu.VMEM((B, B), jnp.bfloat16),
            pltpu.VMEM((ROWS, B), jnp.bfloat16),
            pltpu.VMEM((ROWS, B), jnp.bfloat16),
            pltpu.VMEM((3, B, B), jnp.float32),
            pltpu.SemaphoreType.DMA((5,)),
        ],
        compiler_params=pltpu.CompilerParams(vmem_limit_bytes=16 << 20),
        cost_estimate=pl.CostEstimate(flops=18 * 2 * B**3, bytes_accessed=6 << 20, transcendentals=0),
    )(decays, refresh, *arrays)


def places():
    return {name: lax.axis_index(name) for name in EVERY}


def cut_kernel(order, cotangents, activations, *rest):
    outs, other, held, sem = rest[: len(order)], rest[-3], rest[-2], rest[-1]
    at = places()
    spot = (at["y"], at["x_hi"] * 2 + at["x_lo"])
    copies = []

    def copy(src, dst):
        copies.append(pltpu.make_async_copy(src, dst, sem.at[len(copies)]))
        copies[-1].start()

    copy(activations, held)
    pieces = [(at["core"], out) for out in outs] + [(1 - at["core"], other.at[i]) for i in range(len(order))]
    for (core, out), k in zip(pieces, order * 2):
        for j in range(4):
            start = jnp.where(
                core == 0,
                lax.rem(spot[0] + k, 4) * (4 * B) + j * HALF,
                lax.rem(spot[1] + k, 4) * HALF + (4 * j + 2) * B,
            )
            columns = pl.ds(pl.multiple_of(start, HALF), HALF)
            copy(cotangents.at[:, columns], out.at[:, j * HALF : (j + 1) * HALF])
    copies[0].wait()
    for core, out in pieces:
        out[:, 2 * B :] = held[...]
    for c in copies[1:]:
        c.wait()


def cut(order, cotangents, activations):
    free = pl.BlockSpec(memory_space=pltpu.HBM)
    cotangents = pltpu.with_memory_space_constraint(cotangents, pltpu.HBM)
    activations = pltpu.with_memory_space_constraint(activations, pltpu.HBM)
    n = len(order)
    return pl.pallas_call(
        functools.partial(cut_kernel, order),
        name=f"cut_{n}",
        out_shape=(jax.ShapeDtypeStruct((TOKENS, WIDE), jnp.bfloat16),) * n
        + (jax.ShapeDtypeStruct((n, TOKENS, WIDE), jnp.bfloat16),),
        in_specs=[free, free],
        out_specs=(VMEM,) * (n + 1),
        scratch_shapes=[pltpu.VMEM((TOKENS, B), jnp.bfloat16), pltpu.SemaphoreType.DMA((8 * n + 1,))],
        compiler_params=pltpu.CompilerParams(vmem_limit_bytes=4 << 20),
        cost_estimate=pl.CostEstimate(flops=0, bytes_accessed=n << 20, transcendentals=0),
    )(cotangents, activations)


def split_kernel(pieces, *outs):
    for i, out in enumerate(outs):
        out[...] = pieces[i]


def split(pieces):
    return pl.pallas_call(
        split_kernel,
        name="split",
        out_shape=(jax.ShapeDtypeStruct((TOKENS, WIDE), jnp.bfloat16),) * 3,
        in_specs=[VMEM],
        out_specs=(VMEM,) * 3,
        compiler_params=pltpu.CompilerParams(vmem_limit_bytes=1 << 20),
        cost_estimate=pl.CostEstimate(flops=0, bytes_accessed=3 << 20, transcendentals=0),
    )(pieces)


def product_kernel(count, *refs):
    parts, before, outs = refs[:count], refs[count:-4], refs[-4:]
    at = places()
    me = jnp.where(at["core"] == 0, at["x_hi"] * 2 + at["x_lo"], at["y"])
    right = jnp.concatenate([p[:, 2 * B :] for p in parts], axis=0)
    for i, out in enumerate(outs):
        columns = pl.ds(pl.multiple_of(lax.rem(me + ORDER[i], 4) * HALF, HALF), HALF)
        left = jnp.concatenate([p[:, columns] for p in parts], axis=0)
        total = dot(left, right, (0, 0))
        if before:
            total += before[i][...]
        out[...] = total.astype(out.dtype)


def product(parts, before=()):
    send = SEND if before else jnp.float32
    return pl.pallas_call(
        functools.partial(product_kernel, len(parts)),
        name="product",
        out_shape=(jax.ShapeDtypeStruct((HALF, B), send),) * 3 + (jax.ShapeDtypeStruct((HALF, B), jnp.float32),),
        in_specs=[VMEM] * (len(parts) + len(before)),
        out_specs=(VMEM,) * 4,
        compiler_params=pltpu.CompilerParams(vmem_limit_bytes=8 << 20),
        cost_estimate=pl.CostEstimate(flops=len(parts) * B**3, bytes_accessed=4 << 20, transcendentals=0),
    )(*parts, *before)


def plane_sum_kernel(first, second, third, own, keep, near, far):
    total = own[...]
    for part in (first, second, third):
        total += part[...].astype(jnp.float32)
    core = lax.axis_index("core")
    stays = core == lax.axis_index("z_hi")

    @pl.when(core == 0)
    def _():
        keep[...] = total[:ROWS]
        far[...] = total[ROWS:].astype(SEND)

    @pl.when(core == 1)
    def _():
        keep[...] = total[ROWS:]
        far[...] = total[:ROWS].astype(SEND)

    @pl.when(stays)
    def _():
        near[...] = far[...]

    @pl.when(jnp.logical_not(stays))
    def _():
        near[...] = keep[...].astype(SEND)


def plane_sum(parts):
    return pl.pallas_call(
        plane_sum_kernel,
        name="plane_sum",
        out_shape=(
            jax.ShapeDtypeStruct((ROWS, B), jnp.float32),
            jax.ShapeDtypeStruct((ROWS, B), SEND),
            jax.ShapeDtypeStruct((ROWS, B), SEND),
        ),
        in_specs=[VMEM] * 4,
        out_specs=(VMEM,) * 3,
        compiler_params=pltpu.CompilerParams(vmem_limit_bytes=2 << 20),
        cost_estimate=pl.CostEstimate(flops=8 * ROWS * B, bytes_accessed=2 << 20, transcendentals=0),
    )(*parts)


def mirror_sum_kernel(keep, near, far, out):
    stays = lax.axis_index("core") == lax.axis_index("z_hi")

    @pl.when(stays)
    def _():
        out[...] = narrow(keep[...] + near[...].astype(jnp.float32))

    @pl.when(jnp.logical_not(stays))
    def _():
        out[...] = narrow(far[...].astype(jnp.float32) + near[...].astype(jnp.float32))


def mirror_sum(keep, near, far):
    return pl.pallas_call(
        mirror_sum_kernel,
        name="mirror_sum",
        out_shape=jax.ShapeDtypeStruct((ROWS, B), jnp.bfloat16),
        in_specs=[VMEM] * 3,
        out_specs=VMEM,
        compiler_params=pltpu.CompilerParams(vmem_limit_bytes=1 << 20),
        cost_estimate=pl.CostEstimate(flops=2 * ROWS * B, bytes_accessed=1 << 19, transcendentals=0),
    )(keep, near, far)


def quarter_rows(at, a, b):
    top = ((at["x_lo"] ^ a) * 2 + (at["core"] ^ b)) * ROWS
    return pl.ds(pl.multiple_of(top, ROWS), ROWS)


def assemble_kernel(own, p0, p1, p2, p3, full, right):
    at = places()
    for a in range(2):
        for b in range(2):
            pack = (p0, p1, p2, p3)[2 * b + a]
            here = quarter_rows(at, a, b)
            right[here, :] = pack[2]
            for layer in range(2):
                full[layer, here, :] = pack[layer].astype(jnp.float32) if a + b else own[layer]


def assemble(own, packs):
    return pl.pallas_call(
        assemble_kernel,
        name="assemble",
        out_shape=(jax.ShapeDtypeStruct((2, B, B), jnp.float32), jax.ShapeDtypeStruct((B, B), jnp.bfloat16)),
        in_specs=[VMEM] * 5,
        out_specs=(VMEM,) * 2,
        compiler_params=pltpu.CompilerParams(vmem_limit_bytes=1 << 20),
        cost_estimate=pl.CostEstimate(flops=0, bytes_accessed=4 << 20, transcendentals=0),
    )(own, *packs)


def per_device(activations, cotangents, statistics, roots, ages, refresh):
    decays = decay_base ** ages.astype(jnp.float32)
    *own_pieces, other = cut(ORDER[:3], cotangents, activations)
    here, here_other = cut(ORDER[3:], cotangents, activations)
    own_came = [shift(own_pieces[i], True, ORDER[i]) for i in range(3)]
    pieces = split(partner(other, "core"))
    came = [shift(pieces[i], True, ORDER[i]) for i in range(3)]

    early = product([here, partner(here_other, "core")[0]] + own_came)
    *sends, own = product(came, early)
    came = [shift(sends[i], False, ORDER[i]) for i in range(3)]
    pack = jnp.concatenate([narrow(statistics), roots[1:]], axis=0)
    own, pack_core = lax.optimization_barrier((own, partner(pack, "core")))
    keep, near, far = plane_sum(came + [own])
    keep, near, far, pack = lax.optimization_barrier((keep, near, far, pack))
    part = mirror_sum(keep, *mirror(near, far))
    pack_x = partner(pack, "x_lo")
    part = rounded(part.astype(jnp.float32) + swap_z(part, 1).astype(jnp.float32))
    part, pack_x = lax.optimization_barrier((part, pack_x))
    part = rounded(part.astype(jnp.float32) + swap_z(part, 2).astype(jnp.float32))
    part_x, part_core = partner(part, "x_lo"), partner(part, "core")
    grads = (part, part_x, part_core, partner(part_x, "core"))
    full, right = assemble(statistics, (pack, pack_x, pack_core, partner(pack_x, "core")))
    return finish(decays, refresh, *grads, full, right, roots[0])


def solution(mesh):
    split = Mesh(mesh.devices.reshape(4, 4, 2, 2, 2, 2), EVERY)
    placed = (P(EVERY, None), P(EVERY, None), P(None, SHARD, None), P(None, SHARD, None), P(), P())
    return jax.shard_map(
        per_device,
        mesh=split,
        in_specs=placed,
        out_specs=(P(SHARD, None), P(None, SHARD, None), P(None, SHARD, None)),
        check_vma=False,
    )
```

```python
import functools
import math

import jax
import jax.numpy as jnp
from jax import lax
from jax.experimental import pallas as pl
from jax.experimental.pallas import tpu as pltpu
from jax.sharding import Mesh
from jax.sharding import PartitionSpec as P

X = ("x_hi", "x_lo")
Z = ("z_lo", "z_hi")
SHARD = ("y", "z_hi", "x_hi", "x_lo", "core")
EVERY = ("z_lo",) + SHARD

B = 512
ROWS = 128
TOKENS = 128
HALF = B // 2
ORDER = (2, 1, 3, 0)
WIDE = 3 * B
SEND = jnp.bfloat16
VMEM = pl.BlockSpec(memory_space=pltpu.VMEM)

decay_base = 0.9
tiny_term = 1e-06


def shift(x, along_y, by):
    pairs = []
    for y in range(4):
        for x_at in range(4):
            for core in range(2):
                moves_y = (core == 0) == along_y
                to = ((y + by) % 4, x_at) if moves_y else (y, (x_at + by) % 4)
                pairs.append(((y * 4 + x_at) * 2 + core, (to[0] * 4 + to[1]) * 2 + core))
    return lax.ppermute(x, ("y",) + X + ("core",), pairs)


def ring_spot(z):
    return (z % 4) * 2 + z // 4


def between_holders(x, to):
    pairs = []
    for z in range(8):
        for side in range(2):
            z_to, side_to = to(z, side)
            core = z // 4
            pairs.append(((ring_spot(z) * 2 + side) * 2 + core, (ring_spot(z_to) * 2 + side_to) * 2 + core))
    return lax.ppermute(x, Z + ("x_lo", "core"), pairs)


def mirror(x):
    pairs = [(ring_spot(z) * 2 + 1 - z // 4, ring_spot(7 - z) * 2 + 1 - z // 4) for z in range(8)]
    return lax.ppermute(x, Z + ("core",), pairs)


def hand_over(x):
    return lax.ppermute(x, ("z_hi", "core"), [(0, 1), (3, 2)])


def partner(x, axis, bits=1):
    n = lax.axis_size(axis)
    return lax.ppermute(x, axis, [(i, i ^ bits) for i in range(n)])


def dot(a, b, contract=(1, 0)):
    dims = (((contract[0],), (contract[1],)), ((), ()))
    return lax.dot_general(a, b, dims, preferred_element_type=jnp.float32)


def narrow(x):
    return x.astype(jnp.bfloat16)


def rounded(x):
    return lax.optimization_barrier(narrow(x))


def finish_kernel(decays, refresh, held, held_x, given, given_x, old_stats, old_right, left_old,
                  update, new_stats, new_roots, grad, full, right, left, result, work, sem):
    at = places()
    quarter = at["x_lo"] * 2 + at["core"]
    own = quarter_rows(at, 0, 0)
    factor = 2 * (at["y"] * 4 + at["z_hi"] * 2 + at["x_hi"])
    decay = (decays[factor], decays[factor + 1])
    fresh = (refresh[factor], refresh[factor + 1])
    holds = at["core"] == at["z_hi"]

    def place(near, far):
        for i, rows in enumerate((near, far)):
            top = (at["x_lo"] ^ i) * HALF
            grad[pl.ds(pl.multiple_of(top, HALF), HALF), :] = rows[...]

    @pl.when(holds)
    def _():
        place(held, held_x)

    @pl.when(jnp.logical_not(holds))
    def _():
        place(given, given_x)

    g = grad[...]
    writes = []

    def write(i, src, dst):
        writes.append(pltpu.make_async_copy(src, dst, sem.at[i]))
        writes[-1].start()

    def refresh_stats(layer, gram):
        old = old_stats[layer]
        d = decay[layer]
        a = jnp.where(fresh[layer] == 1, d * old + (1.0 - d) * gram, old)
        full[layer] = a
        write(layer, full.at[layer, own, :], new_stats.at[layer])
        total = jnp.sum(jnp.sum(a * a, axis=0, keepdims=True), axis=1, keepdims=True)
        scaling = 2.5 / jnp.sqrt(total + tiny_term)
        return scaling * a, jnp.sqrt(jnp.sqrt(scaling))

    def both(f, *pairs):
        return f(*(p[0] for p in pairs)), f(*(p[1] for p in pairs))

    def advance(m):
        mb = both(narrow, m)
        square = both(dot, mb, mb)
        u = both(lambda s, v: narrow(s * 0.0625 - 0.625 * v), square, m)
        w = both(dot, u, mb)
        wb = both(narrow, w)
        last = both(dot, u, wb)
        return both(lambda v, w, t: 2.44140625 * v + 3.125 * w + t, m, w, last), mb

    def spread(shape, row0):
        r = lax.broadcasted_iota(jnp.int32, shape, 0) + row0
        c = lax.broadcasted_iota(jnp.int32, shape, 1)
        return jnp.where(r == c, 1.953125, 0.0)

    grams = (dot(g, g, (1, 1)), dot(g, g, (0, 0)))
    m, scale = zip(refresh_stats(0, grams[0]), refresh_stats(1, grams[1]))
    work[0] = m[0]
    m2, mb = advance(m)
    work[1] = m2[0]
    m3, m2b = advance(m2)
    work[2] = m3[0]
    m3b = both(narrow, m3)
    rows = [work[i, own, :] for i in range(3)]
    first = (rows[0], m[1]), (rows[1], m2[1]), (rows[2], m3[1])
    product = dot(narrow(rows[0]), m2b[0]), dot(mb[1], m2b[1])
    y = both(lambda p, v, v2: p * 0.0625 - 0.3125 * (v + v2), product, first[0], first[1])
    product = both(dot, both(narrow, y), m3b)
    diagonal = spread((ROWS, B), quarter * ROWS), spread((B, B), 0)
    out = both(
        lambda e, v, v3, p, s: narrow(s * (e + 1.25 * v - 0.390625 * v3 - 0.25 * p)),
        diagonal, y, first[2], product, scale,
    )
    left[...] = jnp.where(fresh[0] == 1, out[0], left_old[...])
    write(2, left, new_roots.at[0])
    right[...] = jnp.where(fresh[1] == 1, out[1], old_right[...])
    write(3, right.at[own, :], new_roots.at[1])
    mixed = narrow(dot(g, right[...]))
    result[...] = narrow(dot(left[...], mixed) * math.sqrt(B))
    write(4, result, update)
    for w in writes:
        w.wait()


def finish(decays, refresh, *arrays):
    smem = pl.BlockSpec(memory_space=pltpu.SMEM)
    return pl.pallas_call(
        finish_kernel,
        name="finish",
        out_shape=(
            jax.ShapeDtypeStruct((ROWS, B), jnp.bfloat16),
            jax.ShapeDtypeStruct((2, ROWS, B), jnp.float32),
            jax.ShapeDtypeStruct((2, ROWS, B), jnp.bfloat16),
        ),
        in_specs=[smem] * 2 + [VMEM] * 7,
        out_specs=(pl.BlockSpec(memory_space=pltpu.HBM),) * 3,
        scratch_shapes=[
            pltpu.VMEM((B, B), jnp.bfloat16),
            pltpu.VMEM((2, B, B), jnp.float32),
            pltpu.VMEM((B, B), jnp.bfloat16),
            pltpu.VMEM((ROWS, B), jnp.bfloat16),
            pltpu.VMEM((ROWS, B), jnp.bfloat16),
            pltpu.VMEM((3, B, B), jnp.float32),
            pltpu.SemaphoreType.DMA((5,)),
        ],
        compiler_params=pltpu.CompilerParams(vmem_limit_bytes=16 << 20),
        cost_estimate=pl.CostEstimate(flops=18 * 2 * B**3, bytes_accessed=6 << 20, transcendentals=0),
    )(decays, refresh, *arrays)


def places():
    return {name: lax.axis_index(name) for name in EVERY}


def cut_kernel(cotangents, activations, *rest):
    outs, other, held, sem = rest[:4], rest[4], rest[5], rest[6]
    at = places()
    spot = (at["y"], at["x_hi"] * 2 + at["x_lo"])
    copies = []

    def copy(src, dst):
        copies.append(pltpu.make_async_copy(src, dst, sem.at[len(copies)]))
        copies[-1].start()

    copy(activations, held)
    pieces = [(at["core"], out) for out in outs] + [(1 - at["core"], other.at[i]) for i in range(4)]
    for (core, out), k in zip(pieces, ORDER * 2):
        for j in range(4):
            start = jnp.where(
                core == 0,
                lax.rem(spot[0] + k, 4) * (4 * B) + j * HALF,
                lax.rem(spot[1] + k, 4) * HALF + (4 * j + 2) * B,
            )
            columns = pl.ds(pl.multiple_of(start, HALF), HALF)
            copy(cotangents.at[:, columns], out.at[:, j * HALF : (j + 1) * HALF])
    copies[0].wait()
    for core, out in pieces:
        out[:, 2 * B :] = held[...]
    for c in copies[1:]:
        c.wait()


def cut(cotangents, activations):
    free = pl.BlockSpec(memory_space=pltpu.HBM)
    cotangents = pltpu.with_memory_space_constraint(cotangents, pltpu.HBM)
    activations = pltpu.with_memory_space_constraint(activations, pltpu.HBM)
    return pl.pallas_call(
        cut_kernel,
        name="cut",
        out_shape=(jax.ShapeDtypeStruct((TOKENS, WIDE), jnp.bfloat16),) * 4
        + (jax.ShapeDtypeStruct((4, TOKENS, WIDE), jnp.bfloat16),),
        in_specs=[free, free],
        out_specs=(VMEM,) * 5,
        scratch_shapes=[pltpu.VMEM((TOKENS, B), jnp.bfloat16), pltpu.SemaphoreType.DMA((33,))],
        compiler_params=pltpu.CompilerParams(vmem_limit_bytes=4 << 20),
        cost_estimate=pl.CostEstimate(flops=0, bytes_accessed=6 << 20, transcendentals=0),
    )(cotangents, activations)


def split_kernel(pieces, *outs):
    for i, out in enumerate(outs):
        out[...] = pieces[i]


def split(pieces):
    return pl.pallas_call(
        split_kernel,
        name="split",
        out_shape=(jax.ShapeDtypeStruct((TOKENS, WIDE), jnp.bfloat16),) * 4,
        in_specs=[VMEM],
        out_specs=(VMEM,) * 4,
        compiler_params=pltpu.CompilerParams(vmem_limit_bytes=1 << 20),
        cost_estimate=pl.CostEstimate(flops=0, bytes_accessed=3 << 20, transcendentals=0),
    )(pieces)


def product_kernel(count, *refs):
    parts, before, outs = refs[:count], refs[count:-4], refs[-4:]
    at = places()
    me = jnp.where(at["core"] == 0, at["x_hi"] * 2 + at["x_lo"], at["y"])
    right = jnp.concatenate([p[:, 2 * B :] for p in parts], axis=0)
    for i, out in enumerate(outs):
        columns = pl.ds(pl.multiple_of(lax.rem(me + ORDER[i], 4) * HALF, HALF), HALF)
        left = jnp.concatenate([p[:, columns] for p in parts], axis=0)
        total = dot(left, right, (0, 0))
        if before:
            total += before[i][...]
        out[...] = total.astype(out.dtype)


def product(parts, before=()):
    send = SEND if before else jnp.float32
    return pl.pallas_call(
        functools.partial(product_kernel, len(parts)),
        name="product",
        out_shape=(jax.ShapeDtypeStruct((HALF, B), send),) * 3 + (jax.ShapeDtypeStruct((HALF, B), jnp.float32),),
        in_specs=[VMEM] * (len(parts) + len(before)),
        out_specs=(VMEM,) * 4,
        compiler_params=pltpu.CompilerParams(vmem_limit_bytes=8 << 20),
        cost_estimate=pl.CostEstimate(flops=len(parts) * B**3, bytes_accessed=4 << 20, transcendentals=0),
    )(*parts, *before)


def plane_sum_kernel(first, second, third, own, total, send):
    t = own[...]
    for part in (first, second, third):
        t += part[...].astype(jnp.float32)
    total[...] = t
    send[...] = t.astype(SEND)


def plane_sum(parts):
    return pl.pallas_call(
        plane_sum_kernel,
        name="plane_sum",
        out_shape=(jax.ShapeDtypeStruct((HALF, B), jnp.float32), jax.ShapeDtypeStruct((HALF, B), SEND)),
        in_specs=[VMEM] * 4,
        out_specs=(VMEM,) * 2,
        compiler_params=pltpu.CompilerParams(vmem_limit_bytes=2 << 20),
        cost_estimate=pl.CostEstimate(flops=8 * ROWS * B, bytes_accessed=2 << 20, transcendentals=0),
    )(*parts)


def quarter_rows(at, a, b):
    top = ((at["x_lo"] ^ a) * 2 + (at["core"] ^ b)) * ROWS
    return pl.ds(pl.multiple_of(top, ROWS), ROWS)


def assemble_kernel(own, own_right, s1, s2, s3, r1, r2, r3, full, right):
    at = places()
    for a in range(2):
        for b in range(2):
            here = quarter_rows(at, a, b)
            right[here, :] = (own_right, r1, r2, r3)[2 * b + a][...]
            for layer in range(2):
                full[layer, here, :] = (own, s1, s2, s3)[2 * b + a][layer].astype(jnp.float32)


def assemble(*arrays):
    return pl.pallas_call(
        assemble_kernel,
        name="assemble",
        out_shape=(jax.ShapeDtypeStruct((2, B, B), jnp.float32), jax.ShapeDtypeStruct((B, B), jnp.bfloat16)),
        in_specs=[VMEM] * 8,
        out_specs=(VMEM,) * 2,
        compiler_params=pltpu.CompilerParams(vmem_limit_bytes=1 << 20),
        cost_estimate=pl.CostEstimate(flops=0, bytes_accessed=4 << 20, transcendentals=0),
    )(*arrays)


def per_device(activations, cotangents, statistics, roots, ages, refresh):
    decays = decay_base ** ages.astype(jnp.float32)
    *own_pieces, other = cut(cotangents, activations)
    own_came = [shift(own_pieces[i], True, ORDER[i]) for i in range(3)]
    pieces = split(partner(other, "core"))
    came = [shift(pieces[i], True, ORDER[i]) for i in range(3)]

    early = product([own_pieces[3], pieces[3]] + own_came)
    *sends, own = product(came, early)
    came = [shift(sends[i], False, ORDER[i]) for i in range(3)]
    stats, right = narrow(statistics), roots[1]
    own, stats_core, right_core = lax.optimization_barrier((own, partner(stats, "core"), partner(right, "core")))
    total, send = plane_sum(came + [own])
    total, send, stats, right = lax.optimization_barrier((total, send, stats, right))
    stats_x, right_x = partner(stats, "x_lo"), partner(right, "x_lo")
    part = rounded(total + mirror(send).astype(jnp.float32))
    part, stats_x = lax.optimization_barrier((part, stats_x))
    part = rounded(part.astype(jnp.float32) + between_holders(part, lambda z, a: (z ^ 1, a)).astype(jnp.float32))
    part, right_x = lax.optimization_barrier((part, right_x))
    part = rounded(part.astype(jnp.float32) + between_holders(part, lambda z, a: (z ^ 2, a)).astype(jnp.float32))
    part_x = between_holders(part, lambda z, a: (z, 1 - a))
    grads = (part, part_x, hand_over(part), hand_over(part_x))
    full, right = assemble(
        statistics, roots[1], stats_x, stats_core, partner(stats_x, "core"), right_x, right_core, partner(right_x, "core")
    )
    return finish(decays, refresh, *grads, full, right, roots[0])


def solution(mesh):
    split = Mesh(mesh.devices.reshape(4, 4, 2, 2, 2, 2), EVERY)
    placed = (P(EVERY, None), P(EVERY, None), P(None, SHARD, None), P(None, SHARD, None), P(), P())
    return jax.shard_map(
        per_device,
        mesh=split,
        in_specs=placed,
        out_specs=(P(SHARD, None), P(None, SHARD, None), P(None, SHARD, None)),
        check_vma=False,
    )
```

```python
import functools
import math

import jax
import jax.numpy as jnp
from jax import lax
from jax.experimental import pallas as pl
from jax.experimental.pallas import tpu as pltpu
from jax.sharding import Mesh
from jax.sharding import PartitionSpec as P

X = ("x_hi", "x_lo")
Z = ("z_lo", "z_hi")
SHARD = ("y", "z_hi", "x_hi", "x_lo", "core")
EVERY = ("z_lo",) + SHARD

B = 512
ROWS = 128
TOKENS = 128
PART = 64
HALF = B // 2
ORDER = (2, 1, 3, 0)
WIDE = 3 * B
SEND = jnp.bfloat16
VMEM = pl.BlockSpec(memory_space=pltpu.VMEM)

decay_base = 0.9
tiny_term = 1e-06


def shift(x, along_y, by):
    pairs = []
    for y in range(4):
        for x_at in range(4):
            for core in range(2):
                moves_y = (core == 0) == along_y
                to = ((y + by) % 4, x_at) if moves_y else (y, (x_at + by) % 4)
                pairs.append(((y * 4 + x_at) * 2 + core, (to[0] * 4 + to[1]) * 2 + core))
    return lax.ppermute(x, ("y",) + X + ("core",), pairs)


def ring_spot(z, core=None):
    spot = (z % 4) * 2 + z // 4
    return spot if core is None else spot * 2 + core


def swap_z(x, bits):
    return lax.ppermute(x, Z, [(ring_spot(z), ring_spot(z ^ bits)) for z in range(8)])


def mirror(near, far):
    first, second = [], []
    for z in range(8):
        stays = z // 4
        across = 7 - z
        first.append((ring_spot(z, stays), ring_spot(z, 1 - stays)))
        first.append((ring_spot(z, 1 - stays), ring_spot(across, 1 - stays)))
        second.append((ring_spot(z, 1 - stays), ring_spot(across, stays)))
    axes = Z + ("core",)
    return lax.ppermute(near, axes, first), lax.ppermute(far, axes, second)


def diagonal(x):
    pairs = [(z * 2 + a, (z ^ 1) * 2 + 1 - a) for z in range(4) for a in range(2)]
    return lax.ppermute(x, ("z_lo", "x_lo"), pairs)


def partner(x, axis, bits=1):
    n = lax.axis_size(axis)
    return lax.ppermute(x, axis, [(i, i ^ bits) for i in range(n)])


def dot(a, b, contract=(1, 0)):
    dims = (((contract[0],), (contract[1],)), ((), ()))
    return lax.dot_general(a, b, dims, preferred_element_type=jnp.float32)


def narrow(x):
    return x.astype(jnp.bfloat16)


def rounded(x):
    return lax.optimization_barrier(narrow(x))


def finish_kernel(decays, refresh, g_own, g_core, old_stats, old_right, left_old,
                  update, new_stats, new_roots, grad, full, right, left, result, work, sem):
    at = places()
    quarter = at["x_lo"] * 2 + at["core"]
    own = quarter_rows(at, 0, 0)
    factor = 2 * (at["y"] * 4 + at["z_hi"] * 2 + at["x_hi"])
    decay = (decays[factor], decays[factor + 1])
    fresh = (refresh[factor], refresh[factor + 1])
    side = lax.rem(at["z_lo"] + at["z_hi"], 2)
    for i in range(4):
        for b, pieces in enumerate((g_own, g_core)):
            top = ((at["x_lo"] ^ (i // 2)) * 2 + (at["core"] ^ b)) * ROWS + (side ^ (i % 2)) * PART
            grad[pl.ds(pl.multiple_of(top, PART), PART), :] = pieces[i]
    g = grad[...]
    writes = []

    def write(i, src, dst):
        writes.append(pltpu.make_async_copy(src, dst, sem.at[i]))
        writes[-1].start()

    def refresh_stats(layer, gram):
        old = old_stats[layer]
        d = decay[layer]
        a = jnp.where(fresh[layer] == 1, d * old + (1.0 - d) * gram, old)
        full[layer] = a
        write(layer, full.at[layer, own, :], new_stats.at[layer])
        total = jnp.sum(jnp.sum(a * a, axis=0, keepdims=True), axis=1, keepdims=True)
        scaling = 2.5 / jnp.sqrt(total + tiny_term)
        return scaling * a, jnp.sqrt(jnp.sqrt(scaling))

    def both(f, *pairs):
        return f(*(p[0] for p in pairs)), f(*(p[1] for p in pairs))

    def advance(m):
        mb = both(narrow, m)
        square = both(dot, mb, mb)
        u = both(lambda s, v: narrow(s * 0.0625 - 0.625 * v), square, m)
        w = both(dot, u, mb)
        wb = both(narrow, w)
        last = both(dot, u, wb)
        return both(lambda v, w, t: 2.44140625 * v + 3.125 * w + t, m, w, last), mb

    def spread(shape, row0):
        r = lax.broadcasted_iota(jnp.int32, shape, 0) + row0
        c = lax.broadcasted_iota(jnp.int32, shape, 1)
        return jnp.where(r == c, 1.953125, 0.0)

    grams = (dot(g, g, (1, 1)), dot(g, g, (0, 0)))
    m, scale = zip(refresh_stats(0, grams[0]), refresh_stats(1, grams[1]))
    work[0] = m[0]
    m2, mb = advance(m)
    work[1] = m2[0]
    m3, m2b = advance(m2)
    work[2] = m3[0]
    m3b = both(narrow, m3)
    rows = [work[i, own, :] for i in range(3)]
    first = (rows[0], m[1]), (rows[1], m2[1]), (rows[2], m3[1])
    product = dot(narrow(rows[0]), m2b[0]), dot(mb[1], m2b[1])
    y = both(lambda p, v, v2: p * 0.0625 - 0.3125 * (v + v2), product, first[0], first[1])
    product = both(dot, both(narrow, y), m3b)
    diagonal = spread((ROWS, B), quarter * ROWS), spread((B, B), 0)
    out = both(
        lambda e, v, v3, p, s: narrow(s * (e + 1.25 * v - 0.390625 * v3 - 0.25 * p)),
        diagonal, y, first[2], product, scale,
    )
    left[...] = jnp.where(fresh[0] == 1, out[0], left_old[...])
    write(2, left, new_roots.at[0])
    right[...] = jnp.where(fresh[1] == 1, out[1], old_right[...])
    write(3, right.at[own, :], new_roots.at[1])
    mixed = narrow(dot(g, right[...]))
    result[...] = narrow(dot(left[...], mixed) * math.sqrt(B))
    write(4, result, update)
    for w in writes:
        w.wait()


def finish(decays, refresh, *arrays):
    smem = pl.BlockSpec(memory_space=pltpu.SMEM)
    return pl.pallas_call(
        finish_kernel,
        name="finish",
        out_shape=(
            jax.ShapeDtypeStruct((ROWS, B), jnp.bfloat16),
            jax.ShapeDtypeStruct((2, ROWS, B), jnp.float32),
            jax.ShapeDtypeStruct((2, ROWS, B), jnp.bfloat16),
        ),
        in_specs=[smem] * 2 + [VMEM] * 5,
        out_specs=(pl.BlockSpec(memory_space=pltpu.HBM),) * 3,
        scratch_shapes=[
            pltpu.VMEM((B, B), jnp.bfloat16),
            pltpu.VMEM((2, B, B), jnp.float32),
            pltpu.VMEM((B, B), jnp.bfloat16),
            pltpu.VMEM((ROWS, B), jnp.bfloat16),
            pltpu.VMEM((ROWS, B), jnp.bfloat16),
            pltpu.VMEM((3, B, B), jnp.float32),
            pltpu.SemaphoreType.DMA((5,)),
        ],
        compiler_params=pltpu.CompilerParams(vmem_limit_bytes=16 << 20),
        cost_estimate=pl.CostEstimate(flops=18 * 2 * B**3, bytes_accessed=6 << 20, transcendentals=0),
    )(decays, refresh, *arrays)


def places():
    return {name: lax.axis_index(name) for name in EVERY}


def cut_kernel(cotangents, activations, *rest):
    outs, other, held, sem = rest[:4], rest[4], rest[5], rest[6]
    at = places()
    spot = (at["y"], at["x_hi"] * 2 + at["x_lo"])
    copies = []

    def copy(src, dst):
        copies.append(pltpu.make_async_copy(src, dst, sem.at[len(copies)]))
        copies[-1].start()

    copy(activations, held)
    pieces = [(at["core"], out) for out in outs] + [(1 - at["core"], other.at[i]) for i in range(4)]
    for (core, out), k in zip(pieces, ORDER * 2):
        for j in range(4):
            start = jnp.where(
                core == 0,
                lax.rem(spot[0] + k, 4) * (4 * B) + j * HALF,
                lax.rem(spot[1] + k, 4) * HALF + (4 * j + 2) * B,
            )
            columns = pl.ds(pl.multiple_of(start, HALF), HALF)
            copy(cotangents.at[:, columns], out.at[:, j * HALF : (j + 1) * HALF])
    copies[0].wait()
    for core, out in pieces:
        out[:, 2 * B :] = held[...]
    for c in copies[1:]:
        c.wait()


def cut(cotangents, activations):
    free = pl.BlockSpec(memory_space=pltpu.HBM)
    cotangents = pltpu.with_memory_space_constraint(cotangents, pltpu.HBM)
    activations = pltpu.with_memory_space_constraint(activations, pltpu.HBM)
    return pl.pallas_call(
        cut_kernel,
        name="cut",
        out_shape=(jax.ShapeDtypeStruct((TOKENS, WIDE), jnp.bfloat16),) * 4
        + (jax.ShapeDtypeStruct((4, TOKENS, WIDE), jnp.bfloat16),),
        in_specs=[free, free],
        out_specs=(VMEM,) * 5,
        scratch_shapes=[pltpu.VMEM((TOKENS, B), jnp.bfloat16), pltpu.SemaphoreType.DMA((33,))],
        compiler_params=pltpu.CompilerParams(vmem_limit_bytes=4 << 20),
        cost_estimate=pl.CostEstimate(flops=0, bytes_accessed=6 << 20, transcendentals=0),
    )(cotangents, activations)


def split_kernel(pieces, *outs):
    for i, out in enumerate(outs):
        out[...] = pieces[i]


def split(pieces):
    return pl.pallas_call(
        split_kernel,
        name="split",
        out_shape=(jax.ShapeDtypeStruct((TOKENS, WIDE), jnp.bfloat16),) * 4,
        in_specs=[VMEM],
        out_specs=(VMEM,) * 4,
        compiler_params=pltpu.CompilerParams(vmem_limit_bytes=1 << 20),
        cost_estimate=pl.CostEstimate(flops=0, bytes_accessed=3 << 20, transcendentals=0),
    )(pieces)


def product_kernel(count, *refs):
    parts, before, outs = refs[:count], refs[count:-4], refs[-4:]
    at = places()
    me = jnp.where(at["core"] == 0, at["x_hi"] * 2 + at["x_lo"], at["y"])
    right = jnp.concatenate([p[:, 2 * B :] for p in parts], axis=0)
    for i, out in enumerate(outs):
        columns = pl.ds(pl.multiple_of(lax.rem(me + ORDER[i], 4) * HALF, HALF), HALF)
        left = jnp.concatenate([p[:, columns] for p in parts], axis=0)
        total = dot(left, right, (0, 0))
        if before:
            total += before[i][...]
        out[...] = total.astype(out.dtype)


def product(parts, before=()):
    send = SEND if before else jnp.float32
    return pl.pallas_call(
        functools.partial(product_kernel, len(parts)),
        name="product",
        out_shape=(jax.ShapeDtypeStruct((HALF, B), send),) * 3 + (jax.ShapeDtypeStruct((HALF, B), jnp.float32),),
        in_specs=[VMEM] * (len(parts) + len(before)),
        out_specs=(VMEM,) * 4,
        compiler_params=pltpu.CompilerParams(vmem_limit_bytes=8 << 20),
        cost_estimate=pl.CostEstimate(flops=len(parts) * B**3, bytes_accessed=4 << 20, transcendentals=0),
    )(*parts, *before)


def plane_sum_kernel(first, second, third, own, keep, send, total):
    t = own[...]
    for part in (first, second, third):
        t += part[...].astype(jnp.float32)
    total[...] = t
    side = lax.rem(lax.axis_index("z_lo") + lax.axis_index("z_hi"), 2)
    for i in range(2):
        here = pl.ds(pl.multiple_of(i * ROWS + side * PART, PART), PART)
        there = pl.ds(pl.multiple_of(i * ROWS + (1 - side) * PART, PART), PART)
        keep[i] = total[here, :]
        send[i] = total[there, :].astype(SEND)


def plane_sum(parts):
    return pl.pallas_call(
        plane_sum_kernel,
        name="plane_sum",
        out_shape=(
            jax.ShapeDtypeStruct((2, PART, B), jnp.float32),
            jax.ShapeDtypeStruct((2, PART, B), SEND),
        ),
        in_specs=[VMEM] * 4,
        out_specs=(VMEM,) * 2,
        scratch_shapes=[pltpu.VMEM((HALF, B), jnp.float32)],
        compiler_params=pltpu.CompilerParams(vmem_limit_bytes=2 << 20),
        cost_estimate=pl.CostEstimate(flops=8 * ROWS * B, bytes_accessed=2 << 20, transcendentals=0),
    )(*parts)


def pair_sum_kernel(keep, came, base, near, far):
    core = lax.axis_index("core")
    mine = keep[core] + came[core].astype(jnp.float32)
    other = (keep[1 - core] + came[1 - core].astype(jnp.float32)).astype(SEND)
    base[...] = mine
    far[...] = other
    stays = core == lax.axis_index("z_hi")

    @pl.when(stays)
    def _():
        near[...] = other

    @pl.when(jnp.logical_not(stays))
    def _():
        near[...] = mine.astype(SEND)


def pair_sum(keep, came):
    return pl.pallas_call(
        pair_sum_kernel,
        name="pair_sum",
        out_shape=(
            jax.ShapeDtypeStruct((PART, B), jnp.float32),
            jax.ShapeDtypeStruct((PART, B), SEND),
            jax.ShapeDtypeStruct((PART, B), SEND),
        ),
        in_specs=[VMEM] * 2,
        out_specs=(VMEM,) * 3,
        compiler_params=pltpu.CompilerParams(vmem_limit_bytes=1 << 20),
        cost_estimate=pl.CostEstimate(flops=2 * ROWS * B, bytes_accessed=1 << 20, transcendentals=0),
    )(keep, came)


def mirror_sum_kernel(base, near, far, out):
    stays = lax.axis_index("core") == lax.axis_index("z_hi")

    @pl.when(stays)
    def _():
        out[...] = narrow(base[...] + near[...].astype(jnp.float32))

    @pl.when(jnp.logical_not(stays))
    def _():
        out[...] = narrow(far[...].astype(jnp.float32) + near[...].astype(jnp.float32))


def mirror_sum(base, near, far):
    return pl.pallas_call(
        mirror_sum_kernel,
        name="mirror_sum",
        out_shape=jax.ShapeDtypeStruct((PART, B), jnp.bfloat16),
        in_specs=[VMEM] * 3,
        out_specs=VMEM,
        compiler_params=pltpu.CompilerParams(vmem_limit_bytes=1 << 20),
        cost_estimate=pl.CostEstimate(flops=2 * PART * B, bytes_accessed=1 << 19, transcendentals=0),
    )(base, near, far)


def stack_kernel(*refs):
    for i, ref in enumerate(refs[:-1]):
        refs[-1][i] = ref[...]


def stack(parts):
    return pl.pallas_call(
        stack_kernel,
        name="stack",
        out_shape=jax.ShapeDtypeStruct((len(parts),) + parts[0].shape, parts[0].dtype),
        in_specs=[VMEM] * len(parts),
        out_specs=VMEM,
        compiler_params=pltpu.CompilerParams(vmem_limit_bytes=1 << 20),
        cost_estimate=pl.CostEstimate(flops=0, bytes_accessed=1 << 19, transcendentals=0),
    )(*parts)


def quarter_rows(at, a, b):
    top = ((at["x_lo"] ^ a) * 2 + (at["core"] ^ b)) * ROWS
    return pl.ds(pl.multiple_of(top, ROWS), ROWS)


def assemble_kernel(own, own_right, s1, s2, s3, r1, r2, r3, full, right):
    at = places()
    for a in range(2):
        for b in range(2):
            here = quarter_rows(at, a, b)
            right[here, :] = (own_right, r1, r2, r3)[2 * b + a][...]
            for layer in range(2):
                full[layer, here, :] = (own, s1, s2, s3)[2 * b + a][layer].astype(jnp.float32)


def assemble(*arrays):
    return pl.pallas_call(
        assemble_kernel,
        name="assemble",
        out_shape=(jax.ShapeDtypeStruct((2, B, B), jnp.float32), jax.ShapeDtypeStruct((B, B), jnp.bfloat16)),
        in_specs=[VMEM] * 8,
        out_specs=(VMEM,) * 2,
        compiler_params=pltpu.CompilerParams(vmem_limit_bytes=1 << 20),
        cost_estimate=pl.CostEstimate(flops=0, bytes_accessed=4 << 20, transcendentals=0),
    )(*arrays)


def per_device(activations, cotangents, statistics, roots, ages, refresh):
    decays = decay_base ** ages.astype(jnp.float32)
    *own_pieces, other = cut(cotangents, activations)
    own_came = [shift(own_pieces[i], True, ORDER[i]) for i in range(3)]
    pieces = split(partner(other, "core"))
    came = [shift(pieces[i], True, ORDER[i]) for i in range(3)]

    early = product([own_pieces[3], pieces[3]] + own_came)
    *sends, own = product(came, early)
    came = [shift(sends[i], False, ORDER[i]) for i in range(3)]
    stats, right = narrow(statistics), roots[1]
    own, stats_core, right_core = lax.optimization_barrier((own, partner(stats, "core"), partner(right, "core")))
    keep, send = plane_sum(came + [own])
    base, near, far = pair_sum(keep, swap_z(send, 1))
    base, near, far, stats, right = lax.optimization_barrier((base, near, far, stats, right))
    stats_x = partner(stats, "x_lo")
    part, stats_x, right = lax.optimization_barrier((mirror_sum(base, *mirror(near, far)), stats_x, right))
    right_x = partner(right, "x_lo")
    part = rounded(part.astype(jnp.float32) + swap_z(part, 2).astype(jnp.float32))
    part, right_x = lax.optimization_barrier((part, right_x))
    part_z, stats_far, right_far = lax.optimization_barrier(
        (swap_z(part, 1), partner(stats_x, "core"), partner(right_x, "core"))
    )
    grad = stack((part, part_z, partner(part, "x_lo"), diagonal(part)))
    grads = (grad, partner(grad, "core"))
    full, right = assemble(
        statistics, roots[1], stats_x, stats_core, stats_far, right_x, right_core, right_far
    )
    return finish(decays, refresh, *grads, full, right, roots[0])


def solution(mesh):
    split = Mesh(mesh.devices.reshape(4, 4, 2, 2, 2, 2), EVERY)
    placed = (P(EVERY, None), P(EVERY, None), P(None, SHARD, None), P(None, SHARD, None), P(), P())
    return jax.shard_map(
        per_device,
        mesh=split,
        in_specs=placed,
        out_specs=(P(SHARD, None), P(None, SHARD, None), P(None, SHARD, None)),
        check_vma=False,
    )
```
